512 devices in a mesh: gx: 32 (over y, x, core), gy: 16 (over z).
Axes of the slice: x: 4, y: 4, z: 16, core: 2. Of those that a mesh axis runs over, the one named last changes fastest.
Arguments:
- test_vectors: float32 [5, 64, 65536], P(None, None, ('gx', 'gy')), may hold values from -1100 to 1100
- face_jacobians: float32 [4, 5, 5], replicated, may hold values from -2.4 to 2.4
- wave_speed: float32 [65536], P(('gx', 'gy')), may hold values from 0.5 to 2
- viscosity: float32 [65536], P(('gx', 'gy')), may hold values from 0.05 to 0.5
- inverse_volume: float32 [65536], P(('gx', 'gy')), may hold values from 0.5 to 2
- connectivity: int32 [4, 65536], P(None, ('gx', 'gy')), may hold values from 0 to 192, as said below
- send_rows: int32 [4, 8192], P(None, ('gx', 'gy')), may hold values from 0 to 127, as said below
- cell_count: int32 [512], P(('gx', 'gy')), may hold values from 64 to 128, as said below
Outputs:
- basis_vectors: float32 [5, 64, 65536], P(None, None, ('gx', 'gy'))
- factor: float32 [64, 64], replicated
The draws below stay inside these ranges and needn't reach their ends.
Inputs may be any that keep to these rules, and one draw needn't show every extreme that they name: `cell_count`: one partition holds exactly 128 live cells and one exactly 64. `send_rows`: entries of partition p's lists name its owned cells below cell_count[p]; list 0 goes to the partition one row lower, 1 one row higher, 2 one column lower, 3 one column higher; every slot is sent, used or not. `connectivity`: an entry below 128 is a live owned cell; 128 + b * 16 + s is slot s of ghost block b, used only where that neighbouring partition exists; 192 is the far field (zero perturbation). How many slots of a block are used varies by partition and direction.
All inputs are finite; a program needn't handle non-finite values.
Results may differ from the reference program's by a relative error of at most 0.0001.
Values sent between devices are 32-bit elements; how exact they have to be, the bound alone decides.
A program may use at most 64 MiB of HBM per device.

```python
import math
import jax
import jax.numpy as jnp
from jax import lax

FIELDS = 5
VECS = 64
FACES = 4
C_MAX = 128
G_SLOTS = 16
PART_ROWS = 32
PART_COLS = 16
PARTS_SIZE = 512
NCELLS = 65536


def live_counts(key):
    subkeys = jax.random.split(jax.random.fold_in(key, 11), 2)
    counts = jax.random.randint(subkeys[0], (PARTS_SIZE,), C_MAX // 2, C_MAX + 1)
    shuffled = jax.random.permutation(subkeys[1], PARTS_SIZE)
    counts = counts.at[shuffled[0]].set(C_MAX).at[shuffled[1]].set(C_MAX // 2)
    return counts.astype(jnp.int32)


def draw_cell_count(key, part):
    return live_counts(key)


def draw_send_rows(key, part):
    counts = live_counts(key)
    subkeys = jax.random.split(jax.random.fold_in(key, 31), 2)
    listed = jax.random.randint(subkeys[0], (FACES, PARTS_SIZE, G_SLOTS), 0, counts[None, :, None])
    forced_slot = jax.random.randint(subkeys[1], (FACES, PARTS_SIZE), 0, G_SLOTS)
    slot_grid = jnp.arange(G_SLOTS, dtype=jnp.int32)[None, None, :]
    listed = jnp.where(slot_grid == forced_slot[:, :, None], counts[None, :, None] - 1, listed)
    return listed.reshape(FACES, PARTS_SIZE * G_SLOTS).astype(jnp.int32)


def draw_connectivity(key, part):
    counts = live_counts(key)
    subkeys = jax.random.split(jax.random.fold_in(key, 47), 6)
    used_slots = jax.random.randint(subkeys[0], (PARTS_SIZE, FACES), max(1, G_SLOTS // 4), G_SLOTS + 1)
    full_part = jax.random.randint(subkeys[1], (), 0, PARTS_SIZE)
    full_face = jax.random.randint(subkeys[2], (), 0, FACES)
    used_slots = used_slots.at[full_part, full_face].set(G_SLOTS)
    face_kind = jax.random.randint(subkeys[3], (FACES, PARTS_SIZE, C_MAX), 0, 10)
    local_index = jax.random.randint(subkeys[4], (FACES, PARTS_SIZE, C_MAX), 0, counts[None, :, None])
    direction = jnp.clip(face_kind - 6, 0, 3)
    part_index = jnp.arange(PARTS_SIZE, dtype=jnp.int32)
    slot_limit = used_slots[part_index[None, :, None], direction]
    slot_index = jax.random.randint(subkeys[5], (FACES, PARTS_SIZE, C_MAX), 0, slot_limit)
    part_row = part_index // PART_COLS
    part_col = part_index % PART_COLS
    exists = jnp.stack([part_row > 0, part_row < PART_ROWS - 1, part_col > 0, part_col < PART_COLS - 1], axis=1)
    exists_here = exists[part_index[None, :, None], direction]
    ghost_index = C_MAX + direction * G_SLOTS + slot_index
    boundary = C_MAX + FACES * G_SLOTS
    neighbors = jnp.where(face_kind < 6, local_index, jnp.where(exists_here, ghost_index, boundary))
    return neighbors.reshape(FACES, PARTS_SIZE * C_MAX).astype(jnp.int32)


def draw_test_vectors(key, part):
    subkeys = jax.random.split(key, 3)
    cell_scale = jnp.exp(jax.random.uniform(subkeys[0], (NCELLS,), jnp.float32, 0.0, math.log(10.0)))
    column_scale = jnp.exp(jax.random.uniform(subkeys[1], (VECS,), jnp.float32, 0.0, math.log(10.0)))
    device_ramp = 3.0 ** (0.5 * (jnp.arange(NCELLS) // C_MAX).astype(jnp.float32) / (PARTS_SIZE - 1))
    base_draw = jax.random.normal(subkeys[2], (FIELDS, VECS, NCELLS), jnp.float32)
    base_draw = jnp.clip(base_draw, -6.0, 6.0)
    scaled = base_draw * (cell_scale * device_ramp)[None, None, :] * column_scale[None, :, None]
    return scaled.astype(jnp.float32)


def shard_levels(key, extent, cuts, low, high):
    def one(position, parts):
        heights = jax.random.uniform(jax.random.fold_in(jax.random.fold_in(key, 6), position), (parts,), jnp.float32, low / len(cuts), high / len(cuts))
        return jnp.repeat(jnp.exp(heights), extent[position] // parts).reshape((-1,) + (1,) * (len(extent) - position - 1))

    factor_of = one(*cuts[0])
    for cut in cuts[1:]:
        factor_of = factor_of * one(*cut)
    return factor_of


def normal_values(own_key, extent, width, bound, kind=jnp.bfloat16):
    return jnp.clip(width * jax.random.normal(own_key, extent, jnp.float32), -bound, bound).astype(kind)


def setup_inputs(seed: int = 0) -> dict:
    seeds = jax.random.split(jax.random.key(seed), 9)
    return {
        "test_vectors": draw_test_vectors(jax.random.fold_in(seeds[8], 71), 0),
        "face_jacobians": normal_values(seeds[1], (FACES, FIELDS, FIELDS), 0.4, 2.4, jnp.float32),
        "wave_speed": jnp.clip(jnp.exp(math.log(2.0) - 1.3862944 * jax.random.uniform(seeds[2], (NCELLS,), jnp.float32) ** shard_levels(seeds[2], (NCELLS,), ((0, 512),), -0.2, 0.2)), 0.5, 2.0),
        "viscosity": jnp.clip(jnp.exp(math.log(0.5) - 2.3025851 * jax.random.uniform(seeds[3], (NCELLS,), jnp.float32) ** shard_levels(seeds[3], (NCELLS,), ((0, 512),), -0.2, 0.2)), 0.05, 0.5),
        "inverse_volume": jnp.clip(jnp.exp(math.log(2.0) - 1.3862944 * jax.random.uniform(seeds[4], (NCELLS,), jnp.float32) ** shard_levels(seeds[4], (NCELLS,), ((0, 512),), -0.2, 0.2)), 0.5, 2.0),
        "connectivity": draw_connectivity(jax.random.fold_in(seeds[8], 71), 0),
        "send_rows": draw_send_rows(jax.random.fold_in(seeds[8], 71), 0),
        "cell_count": draw_cell_count(jax.random.fold_in(seeds[8], 71), 0),
    }


time_step = 0.4

def shifted(blocks, along, forward):
    length = blocks.shape[along]
    zero_block = jnp.zeros_like(lax.slice_in_dim(blocks, 0, 1, axis=along))
    if forward:
        return jnp.concatenate([zero_block, lax.slice_in_dim(blocks, 0, length - 1, axis=along)], axis=along)
    return jnp.concatenate([lax.slice_in_dim(blocks, 1, length, axis=along), zero_block], axis=along)

def take_rows(current, rows):
    return jnp.take(current, rows, axis=2)

def cell_operator(extended, connect, face_jacobians, wave_speed, viscosity, inverse_volume):
    owned_cells = connect.shape[1]
    own_state = extended[:, :, :owned_cells]
    advection = jnp.zeros(own_state.shape, jnp.float32)
    diffusion = jnp.zeros(own_state.shape, jnp.float32)
    for face_index in range(4):
        neighbor = jnp.take(extended, connect[face_index], axis=2)
        advection = advection + jnp.einsum('ij,jvc->ivc', face_jacobians[face_index], neighbor, precision=lax.Precision.HIGHEST)
        diffusion = diffusion + neighbor
    return inverse_volume * (-0.5 * wave_speed * advection + viscosity * (diffusion - 4.0 * own_state))

def apply_operator(current, face_jacobians, wave_speed, viscosity, inverse_volume, connect, sends):
    outgoing = jax.vmap(jax.vmap(take_rows))(current, sends)
    from_lower_row = shifted(outgoing[:, :, :, :, 1, :], 0, True)
    from_upper_row = shifted(outgoing[:, :, :, :, 0, :], 0, False)
    from_lower_col = shifted(outgoing[:, :, :, :, 3, :], 1, True)
    from_upper_col = shifted(outgoing[:, :, :, :, 2, :], 1, False)
    zero_block = jnp.zeros(current.shape[:4] + (1,), jnp.float32)
    extended = jnp.concatenate([current, from_lower_row, from_upper_row, from_lower_col, from_upper_col, zero_block], axis=4)

    def row_operator(inputs):
        ext_row, conn_row, speed_row, visc_row, volume_row = inputs
        return jax.vmap(cell_operator, in_axes=(0, 0, None, 0, 0, 0))(ext_row, conn_row, face_jacobians, speed_row, visc_row, volume_row)
    return lax.map(row_operator, (extended, connect, wave_speed, viscosity, inverse_volume))

def reference(test_vectors, face_jacobians, wave_speed, viscosity, inverse_volume, connectivity, send_rows, cell_count):
    current = test_vectors.reshape(FIELDS, VECS, PART_ROWS, PART_COLS, C_MAX).transpose(2, 3, 0, 1, 4)
    connect = connectivity.reshape(FACES, PART_ROWS, PART_COLS, C_MAX).transpose(1, 2, 0, 3)
    sends = send_rows.reshape(FACES, PART_ROWS, PART_COLS, G_SLOTS).transpose(1, 2, 0, 3)
    speed_cells = wave_speed.reshape(PART_ROWS, PART_COLS, C_MAX)[:, :, None, None, :]
    visc_cells = viscosity.reshape(PART_ROWS, PART_COLS, C_MAX)[:, :, None, None, :]
    volume_cells = inverse_volume.reshape(PART_ROWS, PART_COLS, C_MAX)[:, :, None, None, :]

    def operate(state_now):
        return apply_operator(state_now, face_jacobians, speed_cells, visc_cells, volume_cells, connect, sends)
    section_one = operate(current)
    section_two = operate(current + 0.5 * time_step * section_one)
    section_three = operate(current + 0.5 * time_step * section_two)
    section_four = operate(current + time_step * section_three)
    advanced = current + time_step / 6.0 * (section_one + 2.0 * section_two + 2.0 * section_three + section_four)
    live_mask = (jnp.arange(C_MAX, dtype=jnp.int32)[None, None, :] < cell_count.reshape(PART_ROWS, PART_COLS)[:, :, None]).astype(jnp.float32)
    advanced = advanced * live_mask[:, :, None, None, :]
    gram_whole = jnp.einsum('abfic,abfjc->ij', advanced, advanced, precision=lax.Precision.HIGHEST)
    gram_whole = gram_whole / float(FIELDS * NCELLS)
    lower_factor = jnp.linalg.cholesky(gram_whole)
    inverse_lower = jax.scipy.linalg.solve_triangular(lower_factor, jnp.eye(VECS, dtype=jnp.float32), lower=True)
    basis_out = jnp.einsum('ij,abfjc->abfic', inverse_lower, advanced, precision=lax.Precision.HIGHEST)
    basis_out = basis_out.transpose(2, 3, 0, 1, 4).reshape(FIELDS, VECS, NCELLS)
    return (basis_out, lower_factor.T)
```

```python
import functools

import jax
import jax.numpy as jnp
from jax import lax
from jax.experimental import pallas as pl
from jax.experimental.pallas import tpu as pltpu
from jax.sharding import PartitionSpec as P

time_step = 0.4
F32 = jnp.float32
HIGHEST = lax.Precision.HIGHEST
MESH = pl.DeviceIdType.MESH


def pick(x, idx):
    return jnp.take_along_axis(x, idx, axis=1, mode="promise_in_bounds")


def step_kernel(
    nx,
    ny,
    tv_ref,
    fj_ref,
    ws_ref,
    vi_ref,
    iv_ref,
    cn_ref,
    sr_ref,
    cc_ref,
    adv_ref,
    gram_ref,
    w_ref,
    acc_ref,
    pad_ref,
    send_ref,
    recv_ref,
    rows_ref,
    part_ref,
    mine_ref,
    line_ref,
    done_ref,
    whole_ref,
    halo_send_sem,
    halo_recv_sem,
    scat_send_sem,
    scat_recv_sem,
    line_send_sem,
    line_recv_sem,
    gath_send_sem,
    gath_recv_sem,
):
    gx = lax.axis_index("gx")
    gy = lax.axis_index("gy")

    barrier = pltpu.get_barrier_semaphore()

    def greet_x(o, c):
        pl.semaphore_signal(
            barrier, inc=1, device_id=(lax.rem(gx + o, nx), gy), device_id_type=MESH
        )
        return c

    def greet_y(o, c):
        pl.semaphore_signal(
            barrier, inc=1, device_id=(gx, lax.rem(gy + o, ny)), device_id_type=MESH
        )
        return c

    lax.fori_loop(1, nx, greet_x, 0)
    lax.fori_loop(1, ny, greet_y, 0)

    rows = lax.broadcasted_iota(jnp.int32, (64, 128), 0)
    lanes = lax.broadcasted_iota(jnp.int32, (64, 128), 1)
    lanes8 = lax.broadcasted_iota(jnp.int32, (8, 128), 1)
    group8 = lanes8 >> 4
    turn = ((lanes >> 4) - (rows >> 3)) & 7
    listed = turn >> 1
    spare = (turn & 1) == 1

    pad_ref[...] = jnp.zeros_like(pad_ref)
    pad_ref[0:4, 0:16] = sr_ref[...]
    send_tile = pick(pad_ref[...], lanes8 & 15)
    send_idx = jnp.zeros((64, 128), jnp.int32)
    for k in range(4):
        row = jnp.broadcast_to(send_tile[k : k + 1, :], (64, 128))
        send_idx = jnp.where(listed == k, row, send_idx)

    a_row = -0.5 * ws_ref[...] * iv_ref[...]
    b_row = vi_ref[...] * iv_ref[...]

    w_ref[...] = tv_ref[...]

    pl.semaphore_wait(barrier, nx + ny - 2)

    def halo(s, k):
        step = 1 if k % 2 else -1
        there = (gx + step, gy) if k < 2 else (gx, gy + step)
        return pltpu.make_async_remote_copy(
            src_ref=send_ref.at[s, k],
            dst_ref=recv_ref.at[s, k],
            send_sem=halo_send_sem.at[s, k],
            recv_sem=halo_recv_sem.at[s, k],
            device_id=there,
            device_id_type=MESH,
        )

    sends_to = [gx > 0, gx < nx - 1, gy > 0, gy < ny - 1]
    comes_in = [gx < nx - 1, gx > 0, gy < ny - 1, gy > 0]

    def stage(s, carry):
        scale = jnp.where(
            s == 0,
            F32(time_step / 4),
            jnp.where(s == 1, F32(time_step / 3), jnp.where(s == 2, F32(time_step / 2), F32(time_step))),
        )
        a_fac = jnp.broadcast_to(a_row * scale, (64, 128))
        b_fac = jnp.broadcast_to(b_row * scale, (64, 128))
        for j in range(5):
            x = pick(w_ref[j], send_idx)
            for k in range(4):
                out = x[0:8]
                for g in range(1, 8):
                    out = jnp.where(group8 == (g + 2 * k) % 8, x[8 * g : 8 * g + 8], out)
                send_ref[s, k, j] = out
        for k in range(4):

            @pl.when(sends_to[k])
            def _(k=k):
                halo(s, k).start()

        adv = [None] * 5
        dif = [None] * 5
        for f in range(4):
            conn = jnp.broadcast_to(cn_ref[f : f + 1, :], (64, 128))
            own = conn < 128
            idx = conn & 127
            for j in range(5):
                n = jnp.where(own, pick(w_ref[j], idx), 0.0)
                dif[j] = n if f == 0 else dif[j] + n
                for i in range(5):
                    t = fj_ref[f, i, j] * n
                    adv[i] = t if adv[i] is None else adv[i] + t
        for i in range(5):
            acc_ref[i] = tv_ref[i] + a_fac * adv[i] + b_fac * (dif[i] - 4.0 * w_ref[i])

        for k in range(4):

            @pl.when(comes_in[k])
            def _(k=k):
                halo(s, k).wait_recv()

        adv = [None] * 5
        dif = [None] * 5
        for j in range(5):
            ghost = jnp.zeros((64, 128), F32)
            for k in range(4):
                block = jnp.concatenate([recv_ref[s, k, j]] * 8, axis=0)
                ghost = jnp.where(jnp.logical_and(listed == k, jnp.logical_not(spare)), block, ghost)
            for f in range(4):
                conn = jnp.broadcast_to(cn_ref[f : f + 1, :], (64, 128))
                slot = conn - 128
                there = ((rows >> 3) << 4) + (((slot >> 4) ^ 1) << 5) + (slot & 15)
                empty = ((rows >> 3) << 4) + 16
                ours = jnp.logical_and(conn >= 128, conn < 192)
                idx = jnp.where(ours, there, empty) & 127
                n = pick(ghost, idx)
                dif[j] = n if f == 0 else dif[j] + n
                for i in range(5):
                    t = fj_ref[f, i, j] * n
                    adv[i] = t if adv[i] is None else adv[i] + t
        for i in range(5):
            w_ref[i] = acc_ref[i] + (a_fac * adv[i] + b_fac * dif[i])
        return carry

    lax.fori_loop(0, 4, stage, 0)

    live = lanes < cc_ref[0]
    adv = [jnp.where(live, w_ref[j], 0.0) for j in range(5)]
    for j in range(5):
        adv_ref[j] = adv[j]
    flat = jnp.concatenate(adv, axis=1)
    twice = jnp.concatenate([flat, flat], axis=0)
    low = lax.dot_general(flat[0:32], twice, (((1,), (1,)), ((), ())), precision=HIGHEST, preferred_element_type=F32)
    high = lax.dot_general(flat[32:64], twice, (((1,), (1,)), ((), ())), precision=HIGHEST, preferred_element_type=F32)
    lanes32 = lax.broadcasted_iota(jnp.int32, (32, 128), 1)
    packed = jnp.where(lanes32 < 64, low, high)
    for r in range(32):
        rows_ref[r] = packed[r : r + 1]

    per = 32 // nx

    def scatter(o):
        to = lax.rem(gx + o, nx)
        return pltpu.make_async_remote_copy(
            src_ref=rows_ref.at[pl.ds(to * per, per)],
            dst_ref=part_ref.at[nx - o],
            send_sem=scat_send_sem,
            recv_sem=scat_recv_sem,
            device_id=(to, gy),
            device_id_type=MESH,
        )

    def scatter_start(o, c):
        scatter(o).start()
        return c

    lax.fori_loop(1, nx, scatter_start, 0)
    part_ref[0] = rows_ref[pl.ds(gx * per, per)]
    sized = part_ref.at[pl.ds(1, nx - 1)]
    pltpu.make_async_copy(sized, sized, scat_recv_sem).wait()
    total = part_ref[0]
    for o in range(1, nx):
        total = total + part_ref[o]
    mine_ref[...] = total

    def line(o):
        return pltpu.make_async_remote_copy(
            src_ref=mine_ref,
            dst_ref=line_ref.at[ny - o],
            send_sem=line_send_sem,
            recv_sem=line_recv_sem,
            device_id=(gx, lax.rem(gy + o, ny)),
            device_id_type=MESH,
        )

    def line_start(o, c):
        line(o).start()
        return c

    lax.fori_loop(1, ny, line_start, 0)
    line_ref[0] = total
    sized_line = line_ref.at[pl.ds(1, ny - 1)]
    pltpu.make_async_copy(sized_line, sized_line, line_recv_sem).wait()
    total = line_ref[lax.rem(ny - gy, ny)]
    for z in range(1, ny):
        total = total + line_ref[lax.rem(ny + z - gy, ny)]
    total = total / F32(5 * 128 * nx * ny)
    done_ref[...] = total

    def gather(o):
        return pltpu.make_async_remote_copy(
            src_ref=done_ref,
            dst_ref=whole_ref.at[pl.ds(gx * per, per)],
            send_sem=gath_send_sem,
            recv_sem=gath_recv_sem,
            device_id=(lax.rem(gx + o, nx), gy),
            device_id_type=MESH,
        )

    def gather_start(o, c):
        gather(o).start()
        return c

    lax.fori_loop(1, nx, gather_start, 0)
    whole_ref[pl.ds(gx * per, per)] = total
    sized_whole = whole_ref.at[pl.ds(0, 32 - per)]
    pltpu.make_async_copy(sized_whole, sized_whole, gath_recv_sem).wait()
    for r in range(32):
        gram_ref[r : r + 1, :] = whole_ref[r]

    for s in range(4):
        for k in range(4):

            @pl.when(sends_to[k])
            def _(s=s, k=k):
                halo(s, k).wait_send()

    pltpu.make_async_copy(sized, sized, scat_send_sem).wait()
    pltpu.make_async_copy(sized_line, sized_line, line_send_sem).wait()
    pltpu.make_async_copy(sized_whole, sized_whole, gath_send_sem).wait()


def factor_kernel(adv_ref, gram_ref, basis_ref, factor_ref):
    lanes = lax.broadcasted_iota(jnp.int32, (8, 128), 1)
    subs = lax.broadcasted_iota(jnp.int32, (8, 128), 0)
    left = lanes < 64
    a = []
    for p in range(8):
        g = gram_ref[8 * (p % 4) : 8 * (p % 4) + 8, :]
        if p >= 4:
            g = pltpu.roll(g, 64, axis=1)
        unit = jnp.where(lanes - 64 == subs + 8 * p, 1.0, 0.0).astype(F32)
        a.append(jnp.where(left, g, unit))

    def across(x, c):
        return jnp.broadcast_to(x[:, c : c + 1], (8, 128))

    def down(x, r):
        return jnp.broadcast_to(x[r : r + 1, :], (8, 128))

    done = []
    for p in range(8):
        cols = [[across(a[r], 8 * p + j) for r in range(p, 8)] for j in range(8)]
        pivots = jnp.ones((8, 128), F32)
        for k in range(8):
            row_of = [down(cols[j][0], k) if j >= k else None for j in range(8)]
            pivots = jnp.where(subs == k, row_of[k], pivots)
            inverse = 1.0 / row_of[k]
            whole_row = down(a[p], k)
            for r in range(p, 8):
                m = cols[k][r - p] * inverse
                if r == p:
                    m = jnp.where(subs > k, m, 0.0)
                for j in range(k + 1, 8):
                    cols[j][r - p] = cols[j][r - p] - m * row_of[j]
                a[r] = a[r] - m * whole_row
        done.append(a[p] / jnp.sqrt(pivots))

    both = jnp.concatenate(done, axis=0)
    swapped = pltpu.roll(both, 64, axis=1)
    rows = lax.broadcasted_iota(jnp.int32, (64, 64), 0)
    columns = lax.broadcasted_iota(jnp.int32, (64, 64), 1)
    factor_ref[...] = jnp.where(columns >= rows, both[:, 0:64], 0.0)
    inv = swapped[:, 0:64]
    for j in range(5):
        basis_ref[j] = lax.dot_general(
            inv, adv_ref[j], (((1,), (0,)), ((), ())), precision=HIGHEST, preferred_element_type=F32
        )


def shards(tv, fj, ws, vi, iv, cn, sr, cc):
    nx = lax.axis_size("gx")
    ny = lax.axis_size("gy")
    vmem = pl.BlockSpec(memory_space=pltpu.VMEM)
    smem = pl.BlockSpec(memory_space=pltpu.SMEM)
    per = 32 // nx
    adv, gram = pl.pallas_call(
        functools.partial(step_kernel, nx, ny),
        out_shape=(
            jax.ShapeDtypeStruct((5, 64, 128), F32),
            jax.ShapeDtypeStruct((32, 128), F32),
        ),
        in_specs=[vmem, smem, vmem, vmem, vmem, vmem, vmem, smem],
        out_specs=(vmem, vmem),
        scratch_shapes=[
            pltpu.VMEM((5, 64, 128), F32),
            pltpu.VMEM((5, 64, 128), F32),
            pltpu.VMEM((8, 128), jnp.int32),
            pltpu.VMEM((4, 4, 5, 8, 128), F32),
            pltpu.VMEM((4, 4, 5, 8, 128), F32),
            pltpu.VMEM((32, 1, 128), F32),
            pltpu.VMEM((nx, per, 1, 128), F32),
            pltpu.VMEM((per, 1, 128), F32),
            pltpu.VMEM((ny, per, 1, 128), F32),
            pltpu.VMEM((per, 1, 128), F32),
            pltpu.VMEM((32, 1, 128), F32),
            pltpu.SemaphoreType.DMA((4, 4)),
            pltpu.SemaphoreType.DMA((4, 4)),
            pltpu.SemaphoreType.DMA,
            pltpu.SemaphoreType.DMA,
            pltpu.SemaphoreType.DMA,
            pltpu.SemaphoreType.DMA,
            pltpu.SemaphoreType.DMA,
            pltpu.SemaphoreType.DMA,
        ],
        compiler_params=pltpu.CompilerParams(collective_id=0, has_side_effects=True),
        name="advance_and_gram",
    )(tv, fj, ws.reshape(1, 128), vi.reshape(1, 128), iv.reshape(1, 128), cn, sr, cc)
    return pl.pallas_call(
        factor_kernel,
        out_shape=(
            jax.ShapeDtypeStruct((5, 64, 128), F32),
            jax.ShapeDtypeStruct((64, 64), F32),
        ),
        in_specs=[vmem, vmem],
        out_specs=(vmem, vmem),
        name="factor_and_apply",
    )(adv, gram)


def solution(mesh):
    cells = P(("gx", "gy"))
    placed = (
        P(None, None, ("gx", "gy")),
        P(),
        cells,
        cells,
        cells,
        P(None, ("gx", "gy")),
        P(None, ("gx", "gy")),
        cells,
    )
    return jax.shard_map(
        shards,
        mesh=mesh,
        in_specs=placed,
        out_specs=(P(None, None, ("gx", "gy")), P()),
        check_vma=False,
    )
```

```python
import functools

import jax
import jax.numpy as jnp
from jax import lax
from jax.experimental import pallas as pl
from jax.experimental.pallas import tpu as pltpu
from jax.sharding import PartitionSpec as P

time_step = 0.4
F32 = jnp.float32
HIGHEST = lax.Precision.HIGHEST
MESH = pl.DeviceIdType.MESH


def pick(x, idx):
    return jnp.take_along_axis(x, idx, axis=1, mode="promise_in_bounds")


def step_kernel(
    nx,
    ny,
    tv_hbm,
    fj_hbm,
    ws_hbm,
    vi_hbm,
    iv_hbm,
    cn_hbm,
    sr_hbm,
    cc_ref,
    adv_ref,
    gram_ref,
    tv_ref,
    fj_ref,
    fac_ref,
    cn_ref,
    sr_ref,
    load_sem,
    w_ref,
    acc_ref,
    pad_ref,
    sidx_ref,
    gidx_ref,
    send_ref,
    recv_ref,
    rows_ref,
    part_ref,
    mine_ref,
    line_ref,
    done_ref,
    whole_ref,
    met_x,
    met_y,
    halo_send_sem,
    halo_recv_sem,
    scat_send_sem,
    scat_recv_sem,
    line_send_sem,
    line_recv_sem,
    gath_send_sem,
    gath_recv_sem,
):
    gx = lax.axis_index("gx")
    gy = lax.axis_index("gy")

    def around_x(o):
        return (lax.rem(gx + o + nx, nx), gy)

    def around_y(o):
        return (gx, lax.rem(gy + o + ny, ny))

    barrier = pltpu.get_barrier_semaphore()
    for there in (around_y(1), around_y(-1), around_x(1), around_x(-1)):
        pl.semaphore_signal(barrier, inc=1, device_id=there, device_id_type=MESH)

    loads = [
        pltpu.make_async_copy(src, dst, load_sem.at[k])
        for k, (src, dst) in enumerate(
            (
                (tv_hbm, tv_ref),
                (fj_hbm, fj_ref),
                (ws_hbm, fac_ref.at[0]),
                (vi_hbm, fac_ref.at[1]),
                (iv_hbm, fac_ref.at[2]),
                (cn_hbm, cn_ref),
                (sr_hbm, sr_ref),
            )
        )
    ]
    for k in (6, 5, 0, 2, 3, 4, 1):
        loads[k].start()

    rows = lax.broadcasted_iota(jnp.int32, (64, 128), 0)
    lanes = lax.broadcasted_iota(jnp.int32, (64, 128), 1)
    lanes8 = lax.broadcasted_iota(jnp.int32, (8, 128), 1)
    group8 = lanes8 >> 4
    turn = ((lanes >> 4) - (rows >> 3)) & 7
    base = (rows >> 3) << 4

    pad_ref[...] = jnp.zeros_like(pad_ref)
    loads[6].wait()
    pad_ref[0:4, 0:16] = sr_ref[...]
    send_tile = pick(pad_ref[...], lanes8 & 15)
    send_idx = jnp.zeros((64, 128), jnp.int32)
    for k in range(4):
        row = jnp.broadcast_to(send_tile[k : k + 1, :], (64, 128))
        send_idx = jnp.where((turn >> 1) == k, row, send_idx)
    sidx_ref[...] = send_idx
    loads[5].wait()
    for f in range(4):
        conn = jnp.broadcast_to(cn_ref[f : f + 1, :], (64, 128))
        slot = conn - 128
        there = base + (((slot >> 4) ^ 1) << 5) + (slot & 15)
        ours = jnp.logical_and(conn >= 128, conn < 192)
        gidx_ref[f] = jnp.where(ours, there, base + 16) & 127

    for k in (0, 2, 3, 4, 1):
        loads[k].wait()
    a_row = -0.5 * fac_ref[0] * fac_ref[2]
    b_row = fac_ref[1] * fac_ref[2]
    w_ref[...] = tv_ref[...]

    pl.semaphore_wait(barrier, 4)

    def halo(s, k):
        step = 1 if k % 2 else -1
        there = (gx + step, gy) if k < 2 else (gx, gy + step)
        slot = lax.rem(s, 2)
        return pltpu.make_async_remote_copy(
            src_ref=send_ref.at[slot, k],
            dst_ref=recv_ref.at[slot, k],
            send_sem=halo_send_sem.at[k],
            recv_sem=halo_recv_sem.at[slot, k],
            device_id=there,
            device_id_type=MESH,
        )

    sends_to = [gx > 0, gx < nx - 1, gy > 0, gy < ny - 1]
    comes_in = [gx < nx - 1, gx > 0, gy < ny - 1, gy > 0]

    def by_stage(s, values):
        out = values[3]
        for k in (2, 1, 0):
            out = jnp.where(s == k, values[k], out)
        return out

    def stage(s, carry):
        scale = by_stage(s, [F32(time_step / 4), F32(time_step / 3), F32(time_step / 2), F32(time_step)])
        a_fac = jnp.broadcast_to(a_row * scale, (64, 128))
        b_fac = jnp.broadcast_to(b_row * scale, (64, 128))
        for j in range(5):
            x = pick(w_ref[j], sidx_ref[...])
            for k in range(4):
                out = x[0:8]
                for g in range(1, 8):
                    out = jnp.where(group8 == (g + 2 * k) % 8, x[8 * g : 8 * g + 8], out)
                send_ref[lax.rem(s, 2), k, j] = out
        for k in range(4):

            @pl.when(sends_to[k])
            def _(k=k):
                halo(s, k).start()

        @pl.when(s > 0)
        def _():
            pl.semaphore_wait(met_x.at[s - 1], 2)
            pl.semaphore_wait(met_y.at[s - 1], 2)

        far_x = by_stage(s, [d % nx for d in (1, 2, 4, 8)])
        far_y = by_stage(s, [d % ny for d in (1, 2, 4, 8)])
        for o in (far_x, nx - far_x):
            pl.semaphore_signal(met_x.at[s], inc=1, device_id=around_x(o), device_id_type=MESH)
        for o in (far_y, ny - far_y):
            pl.semaphore_signal(met_y.at[s], inc=1, device_id=around_y(o), device_id_type=MESH)

        adv = [None] * 5
        dif = [None] * 5
        for f in range(4):
            conn = jnp.broadcast_to(cn_ref[f : f + 1, :], (64, 128))
            own = conn < 128
            idx = conn & 127
            for j in range(5):
                n = jnp.where(own, pick(w_ref[j], idx), 0.0)
                dif[j] = n if f == 0 else dif[j] + n
                for i in range(5):
                    t = fj_ref[i, f, j] * n
                    adv[i] = t if adv[i] is None else adv[i] + t
        for i in range(5):
            acc_ref[i] = tv_ref[i] + a_fac * adv[i] + b_fac * (dif[i] - 4.0 * w_ref[i])

        for k in range(4):

            @pl.when(sends_to[k])
            def _(k=k):
                halo(s, k).wait_send()

        for k in range(4):

            @pl.when(comes_in[k])
            def _(k=k):
                halo(s, k).wait_recv()

        adv = [None] * 5
        dif = [None] * 5
        for j in range(5):
            ghost = jnp.zeros((64, 128), F32)
            for k in range(4):
                block = jnp.concatenate([recv_ref[lax.rem(s, 2), k, j]] * 8, axis=0)
                ghost = jnp.where(turn == 2 * k, block, ghost)
            for f in range(4):
                n = pick(ghost, gidx_ref[f])
                dif[j] = n if f == 0 else dif[j] + n
                for i in range(5):
                    t = fj_ref[i, f, j] * n
                    adv[i] = t if adv[i] is None else adv[i] + t
        for i in range(5):
            w_ref[i] = acc_ref[i] + (a_fac * adv[i] + b_fac * dif[i])
        return carry

    lax.fori_loop(0, 4, stage, 0)

    live = lanes < cc_ref[0]
    adv = [jnp.where(live, w_ref[j], 0.0) for j in range(5)]
    for j in range(5):
        adv_ref[j] = adv[j]
    flat = jnp.concatenate(adv, axis=1)
    twice = jnp.concatenate([flat, flat], axis=0)
    low = lax.dot_general(flat[0:32], twice, (((1,), (1,)), ((), ())), precision=HIGHEST, preferred_element_type=F32)
    high = lax.dot_general(flat[32:64], twice, (((1,), (1,)), ((), ())), precision=HIGHEST, preferred_element_type=F32)
    lanes32 = lax.broadcasted_iota(jnp.int32, (32, 128), 1)
    packed = jnp.where(lanes32 < 64, low, high)
    for r in range(32):
        rows_ref[r] = packed[r : r + 1]
    pl.semaphore_wait(met_x.at[3], 2)
    pl.semaphore_wait(met_y.at[3], 2)

    per = 32 // nx
    wide = min(4, nx // 2)
    high = nx // (2 * wide)
    core = lax.rem(gx, 2)
    col = lax.rem(gx // 2, wide)
    row = gx // (2 * wide)
    hops = lambda d, n: min(d, n - d)
    partners = [
        (dy, dx, dc) for dy in range(high) for dx in range(wide) for dc in range(2) if (dy, dx, dc) != (0, 0, 0)
    ]
    partners.sort(key=lambda d: -(2 * hops(d[0], high) + 2 * hops(d[1], wide) + d[2]))

    def partner(dy, dx, dc):
        there = (lax.rem(row + dy, high) * wide + lax.rem(col + dx, wide)) * 2 + lax.rem(core + dc, 2)
        return there

    def slot_of(dy, dx, dc):
        return (((high - dy) % high) * wide + (wide - dx) % wide) * 2 + dc

    for d in partners:
        to = partner(*d)
        pltpu.make_async_remote_copy(
            src_ref=rows_ref.at[pl.ds(to * per, per)],
            dst_ref=part_ref.at[slot_of(*d)],
            send_sem=scat_send_sem,
            recv_sem=scat_recv_sem,
            device_id=(to, gy),
            device_id_type=MESH,
        ).start()
    part_ref[0] = rows_ref[pl.ds(gx * per, per)]
    sized = part_ref.at[pl.ds(1, nx - 1)]
    pltpu.make_async_copy(sized, sized, scat_recv_sem).wait()
    total = part_ref[0]
    for o in range(1, nx):
        total = total + part_ref[o]
    mine_ref[...] = total

    for o in sorted(range(1, ny), key=lambda o: -hops(o, ny)):
        pltpu.make_async_remote_copy(
            src_ref=mine_ref,
            dst_ref=line_ref.at[ny - o],
            send_sem=line_send_sem,
            recv_sem=line_recv_sem,
            device_id=around_y(o),
            device_id_type=MESH,
        ).start()
    line_ref[0] = total
    sized_line = line_ref.at[pl.ds(1, ny - 1)]
    pltpu.make_async_copy(sized_line, sized_line, line_recv_sem).wait()
    total = line_ref[lax.rem(ny - gy, ny)]
    for z in range(1, ny):
        total = total + line_ref[lax.rem(ny + z - gy, ny)]
    total = total / F32(5 * 128 * nx * ny)
    done_ref[...] = total

    for d in partners:
        pltpu.make_async_remote_copy(
            src_ref=done_ref,
            dst_ref=whole_ref.at[pl.ds(gx * per, per)],
            send_sem=gath_send_sem,
            recv_sem=gath_recv_sem,
            device_id=(partner(*d), gy),
            device_id_type=MESH,
        ).start()
    whole_ref[pl.ds(gx * per, per)] = total
    sized_whole = whole_ref.at[pl.ds(0, 32 - per)]
    pltpu.make_async_copy(sized_whole, sized_whole, gath_recv_sem).wait()
    for r in range(32):
        gram_ref[r : r + 1, :] = whole_ref[r]

    pltpu.make_async_copy(sized, sized, scat_send_sem).wait()
    pltpu.make_async_copy(sized_line, sized_line, line_send_sem).wait()
    pltpu.make_async_copy(sized_whole, sized_whole, gath_send_sem).wait()


def factor_kernel(adv_ref, gram_ref, basis_ref, factor_ref):
    lanes = lax.broadcasted_iota(jnp.int32, (8, 128), 1)
    subs = lax.broadcasted_iota(jnp.int32, (8, 128), 0)
    left = lanes < 64
    a = []
    for p in range(8):
        g = gram_ref[8 * (p % 4) : 8 * (p % 4) + 8, :]
        if p >= 4:
            g = pltpu.roll(g, 64, axis=1)
        unit = jnp.where(lanes - 64 == subs + 8 * p, 1.0, 0.0).astype(F32)
        a.append(jnp.where(left, g, unit))

    def across(x, c):
        return jnp.broadcast_to(x[:, c : c + 1], (8, 128))

    def down(x, r):
        return jnp.broadcast_to(x[r : r + 1, :], (8, 128))

    done = []
    for p in range(8):
        cols = [[across(a[r], 8 * p + j) for r in range(p, 8)] for j in range(8)]
        pivots = jnp.ones((8, 128), F32)
        for k in range(8):
            row_of = [down(cols[j][0], k) if j >= k else None for j in range(8)]
            pivots = jnp.where(subs == k, row_of[k], pivots)
            inverse = 1.0 / row_of[k]
            whole_row = down(a[p], k)
            for r in range(p, 8):
                m = cols[k][r - p] * inverse
                if r == p:
                    m = jnp.where(subs > k, m, 0.0)
                for j in range(k + 1, 8):
                    cols[j][r - p] = cols[j][r - p] - m * row_of[j]
                a[r] = a[r] - m * whole_row
        done.append(a[p] / jnp.sqrt(pivots))

    both = jnp.concatenate(done, axis=0)
    swapped = pltpu.roll(both, 64, axis=1)
    rows = lax.broadcasted_iota(jnp.int32, (64, 64), 0)
    columns = lax.broadcasted_iota(jnp.int32, (64, 64), 1)
    factor_ref[...] = jnp.where(columns >= rows, both[:, 0:64], 0.0)
    inv = swapped[:, 0:64]
    for j in range(5):
        basis_ref[j] = lax.dot_general(
            inv, adv_ref[j], (((1,), (0,)), ((), ())), precision=HIGHEST, preferred_element_type=F32
        )


def shards(tv, fj, ws, vi, iv, cn, sr, cc):
    nx = lax.axis_size("gx")
    ny = lax.axis_size("gy")
    vmem = pl.BlockSpec(memory_space=pltpu.VMEM)
    per = 32 // nx
    hbm = pl.BlockSpec(memory_space=pltpu.HBM)
    adv, gram = pl.pallas_call(
        functools.partial(step_kernel, nx, ny),
        out_shape=(
            jax.ShapeDtypeStruct((5, 64, 128), F32),
            jax.ShapeDtypeStruct((32, 128), F32),
        ),
        in_specs=[hbm] * 7 + [pl.BlockSpec(memory_space=pltpu.SMEM)],
        out_specs=(vmem, vmem),
        scratch_shapes=[
            pltpu.VMEM((5, 64, 128), F32),
            pltpu.SMEM((5, 4, 5), F32),
            pltpu.VMEM((3, 1, 128), F32),
            pltpu.VMEM((4, 128), jnp.int32),
            pltpu.VMEM((4, 16), jnp.int32),
            pltpu.SemaphoreType.DMA((7,)),
            pltpu.VMEM((5, 64, 128), F32),
            pltpu.VMEM((5, 64, 128), F32),
            pltpu.VMEM((8, 128), jnp.int32),
            pltpu.VMEM((64, 128), jnp.int32),
            pltpu.VMEM((4, 64, 128), jnp.int32),
            pltpu.VMEM((2, 4, 5, 8, 128), F32),
            pltpu.VMEM((2, 4, 5, 8, 128), F32),
            pltpu.VMEM((32, 1, 128), F32),
            pltpu.VMEM((nx, per, 1, 128), F32),
            pltpu.VMEM((per, 1, 128), F32),
            pltpu.VMEM((ny, per, 1, 128), F32),
            pltpu.VMEM((per, 1, 128), F32),
            pltpu.VMEM((32, 1, 128), F32),
            pltpu.SemaphoreType.REGULAR((4,)),
            pltpu.SemaphoreType.REGULAR((4,)),
            pltpu.SemaphoreType.DMA((4,)),
            pltpu.SemaphoreType.DMA((2, 4)),
            pltpu.SemaphoreType.DMA,
            pltpu.SemaphoreType.DMA,
            pltpu.SemaphoreType.DMA,
            pltpu.SemaphoreType.DMA,
            pltpu.SemaphoreType.DMA,
            pltpu.SemaphoreType.DMA,
        ],
        compiler_params=pltpu.CompilerParams(
            collective_id=0, has_side_effects=True, vmem_limit_bytes=8 << 20
        ),
        name="advance_and_gram",
    )(
        *[
            pltpu.with_memory_space_constraint(v, pltpu.HBM)
            for v in (
                tv,
                fj.transpose(1, 0, 2),
                ws.reshape(1, 128),
                vi.reshape(1, 128),
                iv.reshape(1, 128),
                cn,
                sr,
            )
        ],
        cc,
    )
    return pl.pallas_call(
        factor_kernel,
        out_shape=(
            jax.ShapeDtypeStruct((5, 64, 128), F32),
            jax.ShapeDtypeStruct((64, 64), F32),
        ),
        in_specs=[vmem, vmem],
        out_specs=(vmem, vmem),
        compiler_params=pltpu.CompilerParams(vmem_limit_bytes=8 << 20),
        name="factor_and_apply",
    )(adv, gram)


def solution(mesh):
    cells = P(("gx", "gy"))
    placed = (
        P(None, None, ("gx", "gy")),
        P(),
        cells,
        cells,
        cells,
        P(None, ("gx", "gy")),
        P(None, ("gx", "gy")),
        cells,
    )
    return jax.shard_map(
        shards,
        mesh=mesh,
        in_specs=placed,
        out_specs=(P(None, None, ("gx", "gy")), P()),
        check_vma=False,
    )
```

```python
import functools

import jax
import jax.numpy as jnp
from jax import lax
from jax.experimental import pallas as pl
from jax.experimental.pallas import tpu as pltpu
from jax.sharding import PartitionSpec as P

time_step = 0.4
F32 = jnp.float32
HIGHEST = lax.Precision.HIGHEST
MESH = pl.DeviceIdType.MESH


def pick(x, idx):
    return jnp.take_along_axis(x, idx, axis=1, mode="promise_in_bounds")


def step_kernel(
    nx,
    ny,
    tv_hbm,
    fj_hbm,
    ws_hbm,
    vi_hbm,
    iv_hbm,
    cn_hbm,
    sr_hbm,
    cc_ref,
    adv_ref,
    gram_ref,
    tv_ref,
    fj_ref,
    fac_ref,
    cn_ref,
    sr_ref,
    load_sem,
    w_ref,
    acc_ref,
    pad_ref,
    sidx_ref,
    gidx_ref,
    send_ref,
    recv_ref,
    rows_ref,
    part_ref,
    mine_ref,
    line_ref,
    done_ref,
    whole_ref,
    met_x,
    met_y,
    halo_send_sem,
    halo_recv_sem,
    scat_send_sem,
    scat_recv_sem,
    line_send_sem,
    line_recv_sem,
    gath_send_sem,
    gath_recv_sem,
):
    gx = lax.axis_index("gx")
    gy = lax.axis_index("gy")

    def around_x(o):
        return (lax.rem(gx + o + nx, nx), gy)

    def around_y(o):
        return (gx, lax.rem(gy + o + ny, ny))

    block = 8 if nx == 32 else 4
    high = nx // block
    place = lax.rem(gx, block)
    row = gx // block

    barrier = pltpu.get_barrier_semaphore()
    for there in (around_y(1), around_y(-1), around_x(1), around_x(-1)):
        pl.semaphore_signal(barrier, inc=1, device_id=there, device_id_type=MESH)

    loads = [
        pltpu.make_async_copy(src, dst, load_sem.at[k])
        for k, (src, dst) in enumerate(
            (
                (tv_hbm, tv_ref),
                (fj_hbm, fj_ref),
                (ws_hbm, fac_ref.at[0]),
                (vi_hbm, fac_ref.at[1]),
                (iv_hbm, fac_ref.at[2]),
                (cn_hbm, cn_ref),
                (sr_hbm, sr_ref),
            )
        )
    ]
    for k in (6, 5, 0, 2, 3, 4, 1):
        loads[k].start()

    rows = lax.broadcasted_iota(jnp.int32, (64, 128), 0)
    lanes = lax.broadcasted_iota(jnp.int32, (64, 128), 1)
    lanes8 = lax.broadcasted_iota(jnp.int32, (8, 128), 1)
    group8 = lanes8 >> 4
    turn = ((lanes >> 4) - (rows >> 3)) & 7
    base = (rows >> 3) << 4

    pad_ref[...] = jnp.zeros_like(pad_ref)
    loads[6].wait()
    pad_ref[0:4, 0:16] = sr_ref[...]
    send_tile = pick(pad_ref[...], lanes8 & 15)
    send_idx = jnp.zeros((64, 128), jnp.int32)
    for k in range(4):
        tiled = jnp.broadcast_to(send_tile[k : k + 1, :], (64, 128))
        send_idx = jnp.where((turn >> 1) == k, tiled, send_idx)
    sidx_ref[...] = send_idx
    loads[5].wait()
    for f in range(4):
        conn = jnp.broadcast_to(cn_ref[f : f + 1, :], (64, 128))
        slot = conn - 128
        there = base + (((slot >> 4) ^ 1) << 5) + (slot & 15)
        ours = jnp.logical_and(conn >= 128, conn < 192)
        gidx_ref[f] = jnp.where(ours, there, base + 16) & 127

    for k in (0, 2, 3, 4, 1):
        loads[k].wait()
    a_row = -0.5 * fac_ref[0] * fac_ref[2]
    b_row = fac_ref[1] * fac_ref[2]
    w_ref[...] = tv_ref[...]

    pl.semaphore_wait(barrier, 4)

    def halo(s, k):
        step = 1 if k % 2 else -1
        there = (gx + step, gy) if k < 2 else (gx, gy + step)
        slot = lax.rem(s, 2)
        return pltpu.make_async_remote_copy(
            src_ref=send_ref.at[slot, k],
            dst_ref=recv_ref.at[slot, k],
            send_sem=halo_send_sem.at[k],
            recv_sem=halo_recv_sem.at[slot, k],
            device_id=there,
            device_id_type=MESH,
        )

    sends_to = [gx > 0, gx < nx - 1, gy > 0, gy < ny - 1]
    comes_in = [gx < nx - 1, gx > 0, gy < ny - 1, gy > 0]

    def by_stage(s, values):
        out = values[3]
        for k in (2, 1, 0):
            out = jnp.where(s == k, values[k], out)
        return out

    def stage(s, carry):
        scale = by_stage(s, [F32(time_step / 4), F32(time_step / 3), F32(time_step / 2), F32(time_step)])
        a_fac = jnp.broadcast_to(a_row * scale, (64, 128))
        b_fac = jnp.broadcast_to(b_row * scale, (64, 128))
        for j in range(5):
            x = pick(w_ref[j], sidx_ref[...])
            for k in range(4):
                out = x[0:8]
                for g in range(1, 8):
                    out = jnp.where(group8 == (g + 2 * k) % 8, x[8 * g : 8 * g + 8], out)
                send_ref[lax.rem(s, 2), k, j] = out
        for k in range(4):

            @pl.when(sends_to[k])
            def _(k=k):
                halo(s, k).start()

        @pl.when(s > 0)
        def _():
            pl.semaphore_wait(met_x.at[s - 1], 2)
            pl.semaphore_wait(met_y.at[s - 1], 2)

        far_x = by_stage(s, [d % nx for d in (1, 2, 4, block)])
        far_y = by_stage(s, [d % ny for d in (1, 2, 4, 8)])
        for o in (far_x, nx - far_x):
            pl.semaphore_signal(met_x.at[s], inc=1, device_id=around_x(o), device_id_type=MESH)
        for o in (far_y, ny - far_y):
            pl.semaphore_signal(met_y.at[s], inc=1, device_id=around_y(o), device_id_type=MESH)

        adv = [None] * 5
        dif = [None] * 5
        for f in range(4):
            conn = jnp.broadcast_to(cn_ref[f : f + 1, :], (64, 128))
            own = conn < 128
            idx = conn & 127
            for j in range(5):
                n = jnp.where(own, pick(w_ref[j], idx), 0.0)
                dif[j] = n if f == 0 else dif[j] + n
                for i in range(5):
                    t = fj_ref[i, f, j] * n
                    adv[i] = t if adv[i] is None else adv[i] + t
        for i in range(5):
            acc_ref[i] = tv_ref[i] + a_fac * adv[i] + b_fac * (dif[i] - 4.0 * w_ref[i])

        for k in range(4):

            @pl.when(sends_to[k])
            def _(k=k):
                halo(s, k).wait_send()

        for k in range(4):

            @pl.when(comes_in[k])
            def _(k=k):
                halo(s, k).wait_recv()

        for h in range(4):
            at = pl.ds(16 * h, 16)
            wheel = turn[16 * h : 16 * h + 16]
            ghosts = []
            for j in range(5):
                ghost = jnp.zeros((16, 128), F32)
                for k in range(4):
                    one = recv_ref[lax.rem(s, 2), k, j]
                    ghost = jnp.where(wheel == 2 * k, jnp.concatenate([one, one], axis=0), ghost)
                ghosts.append(ghost)
            adv = [None] * 5
            dif = [None] * 5
            for f in range(4):
                idx = gidx_ref[f, at]
                for j in range(5):
                    n = pick(ghosts[j], idx)
                    dif[j] = n if f == 0 else dif[j] + n
                    for i in range(5):
                        t = fj_ref[i, f, j] * n
                        adv[i] = t if adv[i] is None else adv[i] + t
            for i in range(5):
                w_ref[i, at] = acc_ref[i, at] + (a_fac[0:16] * adv[i] + b_fac[0:16] * dif[i])
        return carry

    lax.fori_loop(0, 4, stage, 0)

    live = lanes < cc_ref[0]
    adv = [jnp.where(live, w_ref[j], 0.0) for j in range(5)]
    for j in range(5):
        adv_ref[j] = adv[j]
    pl.semaphore_wait(met_x.at[3], 2)
    pl.semaphore_wait(met_y.at[3], 2)
    for o in (block, nx - block):
        pl.semaphore_signal(met_x.at[4], inc=1, device_id=around_x(o), device_id_type=MESH)

    flat = jnp.concatenate(adv, axis=1)
    gram = lax.dot_general(flat, flat, (((1,), (1,)), ((), ())), precision=HIGHEST, preferred_element_type=F32)
    packed = jnp.concatenate([gram[0:32], gram[32:64]], axis=1)
    per = 32 // block
    for r in range(block):
        rows_ref[r] = packed[per * r : per * r + per]

    hops = lambda d, n: min(d, n - d)

    def mate(o):
        core = lax.rem(lax.rem(place, 2) + o, 2)
        col = lax.rem(place // 2 + o // 2, block // 2)
        return col * 2 + core

    mates = sorted(range(1, block), key=lambda o: -hops(o // 2, block // 2))

    for o in mates:
        to = mate(o)
        pltpu.make_async_remote_copy(
            src_ref=rows_ref.at[to],
            dst_ref=part_ref.at[place],
            send_sem=scat_send_sem,
            recv_sem=scat_recv_sem,
            device_id=(row * block + to, gy),
            device_id_type=MESH,
        ).start()
    part_ref[place] = rows_ref[place]
    sized = part_ref.at[pl.ds(1, block - 1)]
    pltpu.make_async_copy(sized, sized, scat_recv_sem).wait()

    def tree(parts):
        while len(parts) > 1:
            parts = [parts[k] + parts[k + 1] if k + 1 < len(parts) else parts[k] for k in range(0, len(parts), 2)]
        return parts[0]

    total = tree([part_ref[r] for r in range(block)])
    mine_ref[...] = total
    pl.semaphore_wait(met_x.at[4], 2)

    here = row * ny + gy
    others = [(dy, dz) for dy in range(high) for dz in range(ny) if (dy, dz) != (0, 0)]
    others.sort(key=lambda d: -hops(d[0], high) - hops(d[1], ny))
    for dy, dz in others:
        pltpu.make_async_remote_copy(
            src_ref=mine_ref,
            dst_ref=line_ref.at[here],
            send_sem=line_send_sem,
            recv_sem=line_recv_sem,
            device_id=(lax.rem(row + dy, high) * block + place, lax.rem(gy + dz, ny)),
            device_id_type=MESH,
        ).start()
    line_ref[here] = total
    sized_line = line_ref.at[pl.ds(1, high * ny - 1)]
    pltpu.make_async_copy(sized_line, sized_line, line_recv_sem).wait()
    total = tree([line_ref[z] for z in range(high * ny)])
    total = total / F32(5 * 128 * nx * ny)
    done_ref[...] = total

    for o in mates:
        pltpu.make_async_remote_copy(
            src_ref=done_ref,
            dst_ref=whole_ref.at[place],
            send_sem=gath_send_sem,
            recv_sem=gath_recv_sem,
            device_id=(row * block + mate(o), gy),
            device_id_type=MESH,
        ).start()
    whole_ref[place] = total
    sized_whole = whole_ref.at[pl.ds(1, block - 1)]
    pltpu.make_async_copy(sized_whole, sized_whole, gath_recv_sem).wait()
    for r in range(block):
        gram_ref[per * r : per * r + per, :] = whole_ref[r]

    pltpu.make_async_copy(sized, sized, scat_send_sem).wait()
    pltpu.make_async_copy(sized_line, sized_line, line_send_sem).wait()
    pltpu.make_async_copy(sized_whole, sized_whole, gath_send_sem).wait()


def factor_kernel(adv_ref, gram_ref, basis_ref, factor_ref):
    lanes = lax.broadcasted_iota(jnp.int32, (8, 128), 1)
    subs = lax.broadcasted_iota(jnp.int32, (8, 128), 0)
    left = lanes < 64
    a = []
    for p in range(8):
        g = gram_ref[8 * (p % 4) : 8 * (p % 4) + 8, :]
        if p >= 4:
            g = pltpu.roll(g, 64, axis=1)
        unit = jnp.where(lanes - 64 == subs + 8 * p, 1.0, 0.0).astype(F32)
        a.append(jnp.where(left, g, unit))

    def across(x, c):
        return jnp.broadcast_to(x[:, c : c + 1], (8, 128))

    def down(x, r):
        return jnp.broadcast_to(x[r : r + 1, :], (8, 128))

    done = []
    for p in range(8):
        cols = [[across(a[r], 8 * p + j) for r in range(p, 8)] for j in range(8)]
        pivots = jnp.ones((8, 128), F32)
        for k in range(8):
            row_of = [down(cols[j][0], k) if j >= k else None for j in range(8)]
            pivots = jnp.where(subs == k, row_of[k], pivots)
            inverse = 1.0 / row_of[k]
            whole_row = down(a[p], k)
            for r in range(p, 8):
                m = cols[k][r - p] * inverse
                if r == p:
                    m = jnp.where(subs > k, m, 0.0)
                for j in range(k + 1, 8):
                    cols[j][r - p] = cols[j][r - p] - m * row_of[j]
                a[r] = a[r] - m * whole_row
        done.append(a[p] / jnp.sqrt(pivots))

    both = jnp.concatenate(done, axis=0)
    swapped = pltpu.roll(both, 64, axis=1)
    rows = lax.broadcasted_iota(jnp.int32, (64, 64), 0)
    columns = lax.broadcasted_iota(jnp.int32, (64, 64), 1)
    factor_ref[...] = jnp.where(columns >= rows, both[:, 0:64], 0.0)
    inv = swapped[:, 0:64]
    for j in range(5):
        basis_ref[j] = lax.dot_general(
            inv, adv_ref[j], (((1,), (0,)), ((), ())), precision=HIGHEST, preferred_element_type=F32
        )


def shards(tv, fj, ws, vi, iv, cn, sr, cc):
    nx = lax.axis_size("gx")
    ny = lax.axis_size("gy")
    vmem = pl.BlockSpec(memory_space=pltpu.VMEM)
    block = 8 if nx == 32 else 4
    per = 32 // block
    hbm = pl.BlockSpec(memory_space=pltpu.HBM)
    adv, gram = pl.pallas_call(
        functools.partial(step_kernel, nx, ny),
        out_shape=(
            jax.ShapeDtypeStruct((5, 64, 128), F32),
            jax.ShapeDtypeStruct((32, 128), F32),
        ),
        in_specs=[hbm] * 7 + [pl.BlockSpec(memory_space=pltpu.SMEM)],
        out_specs=(vmem, vmem),
        scratch_shapes=[
            pltpu.VMEM((5, 64, 128), F32),
            pltpu.SMEM((5, 4, 5), F32),
            pltpu.VMEM((3, 1, 128), F32),
            pltpu.VMEM((4, 128), jnp.int32),
            pltpu.VMEM((4, 16), jnp.int32),
            pltpu.SemaphoreType.DMA((7,)),
            pltpu.VMEM((5, 64, 128), F32),
            pltpu.VMEM((5, 64, 128), F32),
            pltpu.VMEM((8, 128), jnp.int32),
            pltpu.VMEM((64, 128), jnp.int32),
            pltpu.VMEM((4, 64, 128), jnp.int32),
            pltpu.VMEM((2, 4, 5, 8, 128), F32),
            pltpu.VMEM((2, 4, 5, 8, 128), F32),
            pltpu.VMEM((block, per, 128), F32),
            pltpu.VMEM((block, per, 128), F32),
            pltpu.VMEM((per, 128), F32),
            pltpu.VMEM((nx // block * ny, per, 128), F32),
            pltpu.VMEM((per, 128), F32),
            pltpu.VMEM((block, per, 128), F32),
            pltpu.SemaphoreType.REGULAR((5,)),
            pltpu.SemaphoreType.REGULAR((4,)),
            pltpu.SemaphoreType.DMA((4,)),
            pltpu.SemaphoreType.DMA((2, 4)),
            pltpu.SemaphoreType.DMA,
            pltpu.SemaphoreType.DMA,
            pltpu.SemaphoreType.DMA,
            pltpu.SemaphoreType.DMA,
            pltpu.SemaphoreType.DMA,
            pltpu.SemaphoreType.DMA,
        ],
        compiler_params=pltpu.CompilerParams(
            collective_id=0, has_side_effects=True, vmem_limit_bytes=8 << 20
        ),
        name="advance_and_gram",
    )(
        *[
            pltpu.with_memory_space_constraint(v, pltpu.HBM)
            for v in (
                tv,
                fj.transpose(1, 0, 2),
                ws.reshape(1, 128),
                vi.reshape(1, 128),
                iv.reshape(1, 128),
                cn,
                sr,
            )
        ],
        cc,
    )
    return pl.pallas_call(
        factor_kernel,
        out_shape=(
            jax.ShapeDtypeStruct((5, 64, 128), F32),
            jax.ShapeDtypeStruct((64, 64), F32),
        ),
        in_specs=[vmem, vmem],
        out_specs=(vmem, vmem),
        compiler_params=pltpu.CompilerParams(vmem_limit_bytes=8 << 20),
        name="factor_and_apply",
    )(adv, gram)


def solution(mesh):
    cells = P(("gx", "gy"))
    placed = (
        P(None, None, ("gx", "gy")),
        P(),
        cells,
        cells,
        cells,
        P(None, ("gx", "gy")),
        P(None, ("gx", "gy")),
        cells,
    )
    return jax.shard_map(
        shards,
        mesh=mesh,
        in_specs=placed,
        out_specs=(P(None, None, ("gx", "gy")), P()),
        check_vma=False,
    )
```

```python
import functools

import jax
import jax.numpy as jnp
from jax import lax
from jax.experimental import pallas as pl
from jax.experimental.pallas import tpu as pltpu
from jax.sharding import PartitionSpec as P

time_step = 0.4
F32 = jnp.float32
HIGHEST = lax.Precision.HIGHEST
MESH = pl.DeviceIdType.MESH


def pick(x, idx):
    return jnp.take_along_axis(x, idx, axis=1, mode="promise_in_bounds")


def step_kernel(
    nx,
    ny,
    tv_hbm,
    fj_hbm,
    ws_hbm,
    vi_hbm,
    iv_hbm,
    cn_hbm,
    sr_hbm,
    cc_ref,
    adv_ref,
    gram_ref,
    tv_ref,
    fj_ref,
    fac_ref,
    cn_ref,
    sr_ref,
    load_sem,
    w_ref,
    acc_ref,
    pad_ref,
    sidx_ref,
    gidx_ref,
    send_ref,
    recv_ref,
    rows_ref,
    part_ref,
    mine_ref,
    line_ref,
    done_ref,
    whole_ref,
    met_x,
    met_y,
    halo_send_sem,
    halo_recv_sem,
    scat_send_sem,
    scat_recv_sem,
    line_send_sem,
    line_recv_sem,
    gath_send_sem,
    gath_recv_sem,
):
    gx = lax.axis_index("gx")
    gy = lax.axis_index("gy")

    def around_x(o):
        return (lax.rem(gx + o + nx, nx), gy)

    def around_y(o):
        return (gx, lax.rem(gy + o + ny, ny))

    block = nx // 4
    place = lax.rem(gx, block)
    row = gx // block
    pair = row // 2
    odd = lax.rem(row, 2)
    flip = pair + odd - 2 * pair * odd
    member = flip * block + place

    barrier = pltpu.get_barrier_semaphore()
    for there in (around_y(1), around_y(-1), around_x(1), around_x(-1)):
        pl.semaphore_signal(barrier, inc=1, device_id=there, device_id_type=MESH)

    loads = [
        pltpu.make_async_copy(src, dst, load_sem.at[k])
        for k, (src, dst) in enumerate(
            (
                (tv_hbm, tv_ref),
                (fj_hbm, fj_ref),
                (ws_hbm, fac_ref.at[0]),
                (vi_hbm, fac_ref.at[1]),
                (iv_hbm, fac_ref.at[2]),
                (cn_hbm, cn_ref),
                (sr_hbm, sr_ref),
            )
        )
    ]
    for k in (6, 5, 0, 2, 3, 4, 1):
        loads[k].start()

    rows = lax.broadcasted_iota(jnp.int32, (64, 128), 0)
    lanes = lax.broadcasted_iota(jnp.int32, (64, 128), 1)
    lanes8 = lax.broadcasted_iota(jnp.int32, (8, 128), 1)
    group8 = lanes8 >> 4
    turn = ((lanes >> 4) - (rows >> 3)) & 7
    base = (rows >> 3) << 4

    pad_ref[...] = jnp.zeros_like(pad_ref)
    loads[6].wait()
    pad_ref[0:4, 0:16] = sr_ref[...]
    send_tile = pick(pad_ref[...], lanes8 & 15)
    send_idx = jnp.zeros((64, 128), jnp.int32)
    for k in range(4):
        tiled = jnp.broadcast_to(send_tile[k : k + 1, :], (64, 128))
        send_idx = jnp.where((turn >> 1) == k, tiled, send_idx)
    sidx_ref[...] = send_idx
    loads[5].wait()
    for f in range(4):
        conn = jnp.broadcast_to(cn_ref[f : f + 1, :], (64, 128))
        slot = conn - 128
        there = base + (((slot >> 4) ^ 1) << 5) + (slot & 15)
        ours = jnp.logical_and(conn >= 128, conn < 192)
        gidx_ref[f] = jnp.where(ours, there, base + 16) & 127

    for k in (0, 2, 3, 4, 1):
        loads[k].wait()
    a_row = -0.5 * fac_ref[0] * fac_ref[2]
    b_row = fac_ref[1] * fac_ref[2]
    w_ref[...] = tv_ref[...]

    pl.semaphore_wait(barrier, 4)

    def halo(s, k):
        step = 1 if k % 2 else -1
        there = (gx + step, gy) if k < 2 else (gx, gy + step)
        slot = lax.rem(s, 2)
        return pltpu.make_async_remote_copy(
            src_ref=send_ref.at[slot, k],
            dst_ref=recv_ref.at[slot, k],
            send_sem=halo_send_sem.at[k],
            recv_sem=halo_recv_sem.at[slot, k],
            device_id=there,
            device_id_type=MESH,
        )

    sends_to = [gx > 0, gx < nx - 1, gy > 0, gy < ny - 1]
    comes_in = [gx < nx - 1, gx > 0, gy < ny - 1, gy > 0]

    def by_stage(s, values):
        out = values[3]
        for k in (2, 1, 0):
            out = jnp.where(s == k, values[k], out)
        return out

    def stage(s, carry):
        scale = by_stage(s, [F32(time_step / 4), F32(time_step / 3), F32(time_step / 2), F32(time_step)])
        a_fac = jnp.broadcast_to(a_row * scale, (64, 128))
        b_fac = jnp.broadcast_to(b_row * scale, (64, 128))
        for j in range(5):
            x = pick(w_ref[j], sidx_ref[...])
            for k in range(4):
                out = x[0:8]
                for g in range(1, 8):
                    out = jnp.where(group8 == (g + 2 * k) % 8, x[8 * g : 8 * g + 8], out)
                send_ref[lax.rem(s, 2), k, j] = out
        for k in range(4):

            @pl.when(sends_to[k])
            def _(k=k):
                halo(s, k).start()

        @pl.when(s > 0)
        def _():
            pl.semaphore_wait(met_x.at[s - 1], 2)
            pl.semaphore_wait(met_y.at[s - 1], 2)

        far_x = by_stage(s, [d % nx for d in (1, 2, 4, block)])
        far_y = by_stage(s, [d % ny for d in (1, 2, 4, 8)])
        for o in (far_x, nx - far_x):
            pl.semaphore_signal(met_x.at[s], inc=1, device_id=around_x(o), device_id_type=MESH)
        for o in (far_y, ny - far_y):
            pl.semaphore_signal(met_y.at[s], inc=1, device_id=around_y(o), device_id_type=MESH)

        adv = [None] * 5
        dif = [None] * 5
        for f in range(4):
            conn = jnp.broadcast_to(cn_ref[f : f + 1, :], (64, 128))
            own = conn < 128
            idx = conn & 127
            for j in range(5):
                n = jnp.where(own, pick(w_ref[j], idx), 0.0)
                dif[j] = n if f == 0 else dif[j] + n
                for i in range(5):
                    t = fj_ref[i, f, j] * n
                    adv[i] = t if adv[i] is None else adv[i] + t
        for i in range(5):
            acc_ref[i] = tv_ref[i] + a_fac * adv[i] + b_fac * (dif[i] - 4.0 * w_ref[i])

        for k in range(4):

            @pl.when(sends_to[k])
            def _(k=k):
                halo(s, k).wait_send()

        for k in range(4):

            @pl.when(comes_in[k])
            def _(k=k):
                halo(s, k).wait_recv()

        for h in range(4):
            at = pl.ds(16 * h, 16)
            wheel = turn[16 * h : 16 * h + 16]
            ghosts = []
            for j in range(5):
                ghost = jnp.zeros((16, 128), F32)
                for k in range(4):
                    one = recv_ref[lax.rem(s, 2), k, j]
                    ghost = jnp.where(wheel == 2 * k, jnp.concatenate([one, one], axis=0), ghost)
                ghosts.append(ghost)
            adv = [None] * 5
            dif = [None] * 5
            for f in range(4):
                idx = gidx_ref[f, at]
                for j in range(5):
                    n = pick(ghosts[j], idx)
                    dif[j] = n if f == 0 else dif[j] + n
                    for i in range(5):
                        t = fj_ref[i, f, j] * n
                        adv[i] = t if adv[i] is None else adv[i] + t
            for i in range(5):
                w_ref[i, at] = acc_ref[i, at] + (a_fac[0:16] * adv[i] + b_fac[0:16] * dif[i])
        return carry

    lax.fori_loop(0, 4, stage, 0)

    live = lanes < cc_ref[0]
    adv = [jnp.where(live, w_ref[j], 0.0) for j in range(5)]
    for j in range(5):
        adv_ref[j] = adv[j]
    flat = jnp.concatenate(adv, axis=1)
    gram = lax.dot_general(flat, flat, (((1,), (1,)), ((), ())), precision=HIGHEST, preferred_element_type=F32)
    packed = jnp.concatenate([gram[0:32], gram[32:64]], axis=1)
    team = 2 * block
    per = 32 // team
    for r in range(team):
        rows_ref[r] = packed[per * r : per * r + per]
    pl.semaphore_wait(met_x.at[3], 2)
    pl.semaphore_wait(met_y.at[3], 2)

    hops = lambda d, n: min(d, n - d)

    def mate(other, dx, dc):
        core = lax.rem(lax.rem(place, 2) + dc, 2)
        col = lax.rem(place // 2 + dx, block // 2)
        at = col * 2 + core
        to_row = row + 1 - 2 * odd if other else row
        to_flip = 1 - flip if other else flip
        return to_flip * block + at, (to_row * block + at, gy)

    mates = [
        (other, dx, dc) for other in range(2) for dx in range(block // 2) for dc in range(2) if (other, dx, dc) != (0, 0, 0)
    ]
    mates.sort(key=lambda d: -d[0] - hops(d[1], block // 2))

    for d in mates:
        to, there = mate(*d)
        pltpu.make_async_remote_copy(
            src_ref=rows_ref.at[to],
            dst_ref=part_ref.at[member],
            send_sem=scat_send_sem,
            recv_sem=scat_recv_sem,
            device_id=there,
            device_id_type=MESH,
        ).start()
    part_ref[member] = rows_ref[member]
    sized = part_ref.at[pl.ds(1, team - 1)]
    pltpu.make_async_copy(sized, sized, scat_recv_sem).wait()

    def tree(parts):
        while len(parts) > 1:
            parts = [parts[k] + parts[k + 1] if k + 1 < len(parts) else parts[k] for k in range(0, len(parts), 2)]
        return parts[0]

    total = tree([part_ref[r] for r in range(team)])
    mine_ref[...] = total

    here = pair * ny + gy
    others = [(dy, dz) for dy in range(2) for dz in range(ny) if (dy, dz) != (0, 0)]
    others.sort(key=lambda d: -d[0] - hops(d[1], ny))
    for dy, dz in others:
        to_row = 3 - row if dy else row
        pltpu.make_async_remote_copy(
            src_ref=mine_ref,
            dst_ref=line_ref.at[here],
            send_sem=line_send_sem,
            recv_sem=line_recv_sem,
            device_id=(to_row * block + place, lax.rem(gy + dz, ny)),
            device_id_type=MESH,
        ).start()
    line_ref[here] = total
    sized_line = line_ref.at[pl.ds(1, 2 * ny - 1)]
    pltpu.make_async_copy(sized_line, sized_line, line_recv_sem).wait()
    total = tree([line_ref[z] for z in range(2 * ny)])
    total = total / F32(5 * 128 * nx * ny)
    done_ref[...] = total

    for d in mates:
        to, there = mate(*d)
        pltpu.make_async_remote_copy(
            src_ref=done_ref,
            dst_ref=whole_ref.at[member],
            send_sem=gath_send_sem,
            recv_sem=gath_recv_sem,
            device_id=there,
            device_id_type=MESH,
        ).start()
    whole_ref[member] = total
    sized_whole = whole_ref.at[pl.ds(1, team - 1)]
    pltpu.make_async_copy(sized_whole, sized_whole, gath_recv_sem).wait()
    for r in range(team):
        gram_ref[per * r : per * r + per, :] = whole_ref[r]

    pltpu.make_async_copy(sized, sized, scat_send_sem).wait()
    pltpu.make_async_copy(sized_line, sized_line, line_send_sem).wait()
    pltpu.make_async_copy(sized_whole, sized_whole, gath_send_sem).wait()


def factor_kernel(adv_ref, gram_ref, basis_ref, factor_ref):
    lanes = lax.broadcasted_iota(jnp.int32, (8, 128), 1)
    subs = lax.broadcasted_iota(jnp.int32, (8, 128), 0)
    left = lanes < 64
    a = []
    for p in range(8):
        g = gram_ref[8 * (p % 4) : 8 * (p % 4) + 8, :]
        if p >= 4:
            g = pltpu.roll(g, 64, axis=1)
        unit = jnp.where(lanes - 64 == subs + 8 * p, 1.0, 0.0).astype(F32)
        a.append(jnp.where(left, g, unit))

    def across(x, c):
        return jnp.broadcast_to(x[:, c : c + 1], (8, 128))

    def down(x, r):
        return jnp.broadcast_to(x[r : r + 1, :], (8, 128))

    done = []
    for p in range(8):
        cols = [[across(a[r], 8 * p + j) for r in range(p, 8)] for j in range(8)]
        pivots = jnp.ones((8, 128), F32)
        for k in range(8):
            row_of = [down(cols[j][0], k) if j >= k else None for j in range(8)]
            pivots = jnp.where(subs == k, row_of[k], pivots)
            inverse = 1.0 / row_of[k]
            whole_row = down(a[p], k)
            for r in range(p, 8):
                m = cols[k][r - p] * inverse
                if r == p:
                    m = jnp.where(subs > k, m, 0.0)
                for j in range(k + 1, 8):
                    cols[j][r - p] = cols[j][r - p] - m * row_of[j]
                a[r] = a[r] - m * whole_row
        done.append(a[p] / jnp.sqrt(pivots))

    both = jnp.concatenate(done, axis=0)
    swapped = pltpu.roll(both, 64, axis=1)
    rows = lax.broadcasted_iota(jnp.int32, (64, 64), 0)
    columns = lax.broadcasted_iota(jnp.int32, (64, 64), 1)
    factor_ref[...] = jnp.where(columns >= rows, both[:, 0:64], 0.0)
    inv = swapped[:, 0:64]
    for j in range(5):
        basis_ref[j] = lax.dot_general(
            inv, adv_ref[j], (((1,), (0,)), ((), ())), precision=HIGHEST, preferred_element_type=F32
        )


def shards(tv, fj, ws, vi, iv, cn, sr, cc):
    nx = lax.axis_size("gx")
    ny = lax.axis_size("gy")
    vmem = pl.BlockSpec(memory_space=pltpu.VMEM)
    block = nx // 4
    team = 2 * block
    per = 32 // team
    hbm = pl.BlockSpec(memory_space=pltpu.HBM)
    adv, gram = pl.pallas_call(
        functools.partial(step_kernel, nx, ny),
        out_shape=(
            jax.ShapeDtypeStruct((5, 64, 128), F32),
            jax.ShapeDtypeStruct((32, 128), F32),
        ),
        in_specs=[hbm] * 7 + [pl.BlockSpec(memory_space=pltpu.SMEM)],
        out_specs=(vmem, vmem),
        scratch_shapes=[
            pltpu.VMEM((5, 64, 128), F32),
            pltpu.SMEM((5, 4, 5), F32),
            pltpu.VMEM((3, 1, 128), F32),
            pltpu.VMEM((4, 128), jnp.int32),
            pltpu.VMEM((4, 16), jnp.int32),
            pltpu.SemaphoreType.DMA((7,)),
            pltpu.VMEM((5, 64, 128), F32),
            pltpu.VMEM((5, 64, 128), F32),
            pltpu.VMEM((8, 128), jnp.int32),
            pltpu.VMEM((64, 128), jnp.int32),
            pltpu.VMEM((4, 64, 128), jnp.int32),
            pltpu.VMEM((2, 4, 5, 8, 128), F32),
            pltpu.VMEM((2, 4, 5, 8, 128), F32),
            pltpu.VMEM((team, per, 128), F32),
            pltpu.VMEM((team, per, 128), F32),
            pltpu.VMEM((per, 128), F32),
            pltpu.VMEM((2 * ny, per, 128), F32),
            pltpu.VMEM((per, 128), F32),
            pltpu.VMEM((team, per, 128), F32),
            pltpu.SemaphoreType.REGULAR((4,)),
            pltpu.SemaphoreType.REGULAR((4,)),
            pltpu.SemaphoreType.DMA((4,)),
            pltpu.SemaphoreType.DMA((2, 4)),
            pltpu.SemaphoreType.DMA,
            pltpu.SemaphoreType.DMA,
            pltpu.SemaphoreType.DMA,
            pltpu.SemaphoreType.DMA,
            pltpu.SemaphoreType.DMA,
            pltpu.SemaphoreType.DMA,
        ],
        compiler_params=pltpu.CompilerParams(
            collective_id=0, has_side_effects=True, vmem_limit_bytes=8 << 20
        ),
        name="advance_and_gram",
    )(
        *[
            pltpu.with_memory_space_constraint(v, pltpu.HBM)
            for v in (
                tv,
                fj.transpose(1, 0, 2),
                ws.reshape(1, 128),
                vi.reshape(1, 128),
                iv.reshape(1, 128),
                cn,
                sr,
            )
        ],
        cc,
    )
    return pl.pallas_call(
        factor_kernel,
        out_shape=(
            jax.ShapeDtypeStruct((5, 64, 128), F32),
            jax.ShapeDtypeStruct((64, 64), F32),
        ),
        in_specs=[vmem, vmem],
        out_specs=(vmem, vmem),
        compiler_params=pltpu.CompilerParams(vmem_limit_bytes=8 << 20),
        name="factor_and_apply",
    )(adv, gram)


def solution(mesh):
    cells = P(("gx", "gy"))
    placed = (
        P(None, None, ("gx", "gy")),
        P(),
        cells,
        cells,
        cells,
        P(None, ("gx", "gy")),
        P(None, ("gx", "gy")),
        cells,
    )
    return jax.shard_map(
        shards,
        mesh=mesh,
        in_specs=placed,
        out_specs=(P(None, None, ("gx", "gy")), P()),
        check_vma=False,
    )
```

```python
import functools

import jax
import jax.numpy as jnp
from jax import lax
from jax.experimental import pallas as pl
from jax.experimental.pallas import tpu as pltpu
from jax.sharding import PartitionSpec as P

time_step = 0.4
F32 = jnp.float32
HIGHEST = lax.Precision.HIGHEST
MESH = pl.DeviceIdType.MESH


def pick(x, idx):
    return jnp.take_along_axis(x, idx, axis=1, mode="promise_in_bounds")


def step_kernel(
    nx,
    ny,
    tv_hbm,
    fj_hbm,
    ws_hbm,
    vi_hbm,
    iv_hbm,
    cn_hbm,
    sr_hbm,
    cc_ref,
    adv_ref,
    gram_ref,
    tv_ref,
    fj_ref,
    fac_ref,
    cn_ref,
    sr_ref,
    load_sem,
    w_ref,
    acc_ref,
    pad_ref,
    sidx_ref,
    gidx_ref,
    coef_ref,
    send_ref,
    recv_ref,
    rows_ref,
    part_ref,
    mine_ref,
    line_ref,
    done_ref,
    whole_ref,
    met_x,
    met_y,
    halo_send_sem,
    halo_recv_sem,
    scat_send_sem,
    scat_recv_sem,
    line_send_sem,
    line_recv_sem,
    gath_send_sem,
    gath_recv_sem,
):
    gx = lax.axis_index("gx")
    gy = lax.axis_index("gy")

    def around_x(o):
        return (lax.rem(gx + o + nx, nx), gy)

    def around_y(o):
        return (gx, lax.rem(gy + o + ny, ny))

    block = nx // 4
    place = lax.rem(gx, block)
    row = gx // block
    pair = row // 2
    odd = lax.rem(row, 2)
    flip = pair + odd - 2 * pair * odd
    member = flip * block + place

    barrier = pltpu.get_barrier_semaphore()
    for there in (around_y(1), around_y(-1), around_x(1), around_x(-1)):
        pl.semaphore_signal(barrier, inc=1, device_id=there, device_id_type=MESH)

    loads = [
        pltpu.make_async_copy(src, dst, load_sem.at[k])
        for k, (src, dst) in enumerate(
            (
                (tv_hbm, tv_ref),
                (fj_hbm, fj_ref),
                (ws_hbm, fac_ref.at[0]),
                (vi_hbm, fac_ref.at[1]),
                (iv_hbm, fac_ref.at[2]),
                (cn_hbm, cn_ref),
                (sr_hbm, sr_ref),
            )
        )
    ]
    for k in (6, 5, 0, 2, 3, 4, 1):
        loads[k].start()

    rows = lax.broadcasted_iota(jnp.int32, (64, 128), 0)
    lanes = lax.broadcasted_iota(jnp.int32, (64, 128), 1)
    lanes8 = lax.broadcasted_iota(jnp.int32, (8, 128), 1)
    group8 = lanes8 >> 4
    turn = ((lanes >> 4) - (rows >> 3)) & 7
    base = (rows >> 3) << 4

    pad_ref[...] = jnp.zeros_like(pad_ref)
    loads[6].wait()
    pad_ref[0:4, 0:16] = sr_ref[...]
    send_tile = pick(pad_ref[...], lanes8 & 15)
    send_idx = jnp.zeros((64, 128), jnp.int32)
    for k in range(4):
        tiled = jnp.broadcast_to(send_tile[k : k + 1, :], (64, 128))
        send_idx = jnp.where((turn >> 1) == k, tiled, send_idx)
    sidx_ref[...] = send_idx
    loads[5].wait()
    for f in range(4):
        conn = jnp.broadcast_to(cn_ref[f : f + 1, :], (64, 128))
        slot = conn - 128
        there = base + (((slot >> 4) ^ 1) << 5) + (slot & 15)
        ours = jnp.logical_and(conn >= 128, conn < 192)
        gidx_ref[f] = jnp.where(ours, there, base + 16) & 127

    for k in (0, 2, 3, 4, 1):
        loads[k].wait()
    a_row = -0.5 * fac_ref[0] * fac_ref[2]
    ratio = jnp.broadcast_to(fac_ref[1] / (-0.5 * fac_ref[0]), (8, 128))
    centre = jnp.broadcast_to(-4.0 * ratio[0:1], (64, 128))
    for f in range(4):
        for i in range(5):
            for j in range(5):
                entry = jnp.full((8, 128), fj_ref[i, f, j], F32)
                coef_ref[f, i, j] = entry + ratio if i == j else entry
    w_ref[...] = tv_ref[...]

    pl.semaphore_wait(barrier, 4)

    def halo(s, k):
        step = 1 if k % 2 else -1
        there = (gx + step, gy) if k < 2 else (gx, gy + step)
        slot = lax.rem(s, 2)
        return pltpu.make_async_remote_copy(
            src_ref=send_ref.at[slot, k],
            dst_ref=recv_ref.at[slot, k],
            send_sem=halo_send_sem.at[k],
            recv_sem=halo_recv_sem.at[slot, k],
            device_id=there,
            device_id_type=MESH,
        )

    sends_to = [gx > 0, gx < nx - 1, gy > 0, gy < ny - 1]
    comes_in = [gx < nx - 1, gx > 0, gy < ny - 1, gy > 0]

    def by_stage(s, values):
        out = values[3]
        for k in (2, 1, 0):
            out = jnp.where(s == k, values[k], out)
        return out

    def stage(s, carry):
        scale = by_stage(s, [F32(time_step / 4), F32(time_step / 3), F32(time_step / 2), F32(time_step)])
        a_fac = jnp.broadcast_to(a_row * scale, (64, 128))
        for j in range(5):
            x = pick(w_ref[j], sidx_ref[...])
            for k in range(4):
                out = x[0:8]
                for g in range(1, 8):
                    out = jnp.where(group8 == (g + 2 * k) % 8, x[8 * g : 8 * g + 8], out)
                send_ref[lax.rem(s, 2), k, j] = out
        for k in range(4):

            @pl.when(sends_to[k])
            def _(k=k):
                halo(s, k).start()

        @pl.when(s > 0)
        def _():
            pl.semaphore_wait(met_x.at[s - 1], 2)
            pl.semaphore_wait(met_y.at[s - 1], 2)

        far_x = by_stage(s, [d % nx for d in (1, 2, 4, block)])
        far_y = by_stage(s, [d % ny for d in (1, 2, 4, 8)])
        for o in (far_x, nx - far_x):
            pl.semaphore_signal(met_x.at[s], inc=1, device_id=around_x(o), device_id_type=MESH)
        for o in (far_y, ny - far_y):
            pl.semaphore_signal(met_y.at[s], inc=1, device_id=around_y(o), device_id_type=MESH)

        adv = [None] * 5
        for f in range(4):
            conn = jnp.broadcast_to(cn_ref[f : f + 1, :], (64, 128))
            own = conn < 128
            idx = conn & 127
            for j in range(5):
                n = jnp.where(own, pick(w_ref[j], idx), 0.0)
                for i in range(5):
                    t = jnp.concatenate([coef_ref[f, i, j]] * 8, axis=0) * n
                    adv[i] = t if adv[i] is None else adv[i] + t
        for i in range(5):
            acc_ref[i] = tv_ref[i] + a_fac * (adv[i] + centre * w_ref[i])

        for k in range(4):

            @pl.when(sends_to[k])
            def _(k=k):
                halo(s, k).wait_send()

        for k in range(4):

            @pl.when(comes_in[k])
            def _(k=k):
                halo(s, k).wait_recv()

        for h in range(64 // 8):
            at = pl.ds(8 * h, 8)
            wheel = turn[8 * h : 8 * h + 8]
            ghosts = []
            for j in range(5):
                ghost = jnp.zeros((8, 128), F32)
                for k in range(4):
                    block_of = jnp.concatenate([recv_ref[lax.rem(s, 2), k, j]] * (8 // 8), axis=0)
                    ghost = jnp.where(wheel == 2 * k, block_of, ghost)
                ghosts.append(ghost)
            adv = [None] * 5
            for f in range(4):
                idx = gidx_ref[f, at]
                for j in range(5):
                    n = pick(ghosts[j], idx)
                    for i in range(5):
                        t = jnp.concatenate([coef_ref[f, i, j]] * (8 // 8), axis=0) * n
                        adv[i] = t if adv[i] is None else adv[i] + t
            for i in range(5):
                w_ref[i, at] = acc_ref[i, at] + a_fac[0:8] * adv[i]
        return carry

    lax.fori_loop(0, 4, stage, 0)

    live = lanes < cc_ref[0]
    adv = [jnp.where(live, w_ref[j], 0.0) for j in range(5)]
    for j in range(5):
        adv_ref[j] = adv[j]
    flat = jnp.concatenate(adv, axis=1)
    gram = lax.dot_general(flat, flat, (((1,), (1,)), ((), ())), precision=HIGHEST, preferred_element_type=F32)
    packed = jnp.concatenate([gram[0:32], gram[32:64]], axis=1)
    team = 2 * block
    per = 32 // team
    for r in range(team):
        rows_ref[r] = packed[per * r : per * r + per]
    pl.semaphore_wait(met_x.at[3], 2)
    pl.semaphore_wait(met_y.at[3], 2)

    hops = lambda d, n: min(d, n - d)

    def mate(other, dx, dc):
        core = lax.rem(lax.rem(place, 2) + dc, 2)
        col = lax.rem(place // 2 + dx, block // 2)
        at = col * 2 + core
        to_row = row + 1 - 2 * odd if other else row
        to_flip = 1 - flip if other else flip
        return to_flip * block + at, (to_row * block + at, gy)

    mates = [
        (other, dx, dc) for other in range(2) for dx in range(block // 2) for dc in range(2) if (other, dx, dc) != (0, 0, 0)
    ]
    mates.sort(key=lambda d: -d[0] - hops(d[1], block // 2))

    for d in mates:
        to, there = mate(*d)
        pltpu.make_async_remote_copy(
            src_ref=rows_ref.at[to],
            dst_ref=part_ref.at[member],
            send_sem=scat_send_sem,
            recv_sem=scat_recv_sem,
            device_id=there,
            device_id_type=MESH,
        ).start()
    part_ref[member] = rows_ref[member]
    sized = part_ref.at[pl.ds(1, team - 1)]
    pltpu.make_async_copy(sized, sized, scat_recv_sem).wait()

    def tree(parts):
        while len(parts) > 1:
            parts = [parts[k] + parts[k + 1] if k + 1 < len(parts) else parts[k] for k in range(0, len(parts), 2)]
        return parts[0]

    total = tree([part_ref[r] for r in range(team)])
    mine_ref[...] = total

    here = pair * ny + gy
    others = [(dy, dz) for dy in range(2) for dz in range(ny) if (dy, dz) != (0, 0)]
    others.sort(key=lambda d: -d[0] - hops(d[1], ny))
    for dy, dz in others:
        to_row = 3 - row if dy else row
        pltpu.make_async_remote_copy(
            src_ref=mine_ref,
            dst_ref=line_ref.at[here],
            send_sem=line_send_sem,
            recv_sem=line_recv_sem,
            device_id=(to_row * block + place, lax.rem(gy + dz, ny)),
            device_id_type=MESH,
        ).start()
    line_ref[here] = total
    sized_line = line_ref.at[pl.ds(1, 2 * ny - 1)]
    pltpu.make_async_copy(sized_line, sized_line, line_recv_sem).wait()
    total = tree([line_ref[z] for z in range(2 * ny)])
    total = total / F32(5 * 128 * nx * ny)
    done_ref[...] = total

    for d in mates:
        to, there = mate(*d)
        pltpu.make_async_remote_copy(
            src_ref=done_ref,
            dst_ref=whole_ref.at[member],
            send_sem=gath_send_sem,
            recv_sem=gath_recv_sem,
            device_id=there,
            device_id_type=MESH,
        ).start()
    whole_ref[member] = total
    sized_whole = whole_ref.at[pl.ds(1, team - 1)]
    pltpu.make_async_copy(sized_whole, sized_whole, gath_recv_sem).wait()
    for r in range(team):
        gram_ref[per * r : per * r + per, :] = whole_ref[r]

    pltpu.make_async_copy(sized, sized, scat_send_sem).wait()
    pltpu.make_async_copy(sized_line, sized_line, line_send_sem).wait()
    pltpu.make_async_copy(sized_whole, sized_whole, gath_send_sem).wait()


def factor_kernel(adv_ref, gram_ref, basis_ref, factor_ref):
    lanes = lax.broadcasted_iota(jnp.int32, (8, 128), 1)
    subs = lax.broadcasted_iota(jnp.int32, (8, 128), 0)
    left = lanes < 64
    a = []
    for p in range(8):
        g = gram_ref[8 * (p % 4) : 8 * (p % 4) + 8, :]
        if p >= 4:
            g = pltpu.roll(g, 64, axis=1)
        unit = jnp.where(lanes - 64 == subs + 8 * p, 1.0, 0.0).astype(F32)
        a.append(jnp.where(left, g, unit))

    def across(x, c):
        return jnp.broadcast_to(x[:, c : c + 1], (8, 128))

    def down(x, r):
        return jnp.broadcast_to(x[r : r + 1, :], (8, 128))

    done = []
    for p in range(8):
        cols = [[across(a[r], 8 * p + j) for r in range(p, 8)] for j in range(8)]
        pivots = jnp.ones((8, 128), F32)
        for k in range(8):
            row_of = [down(cols[j][0], k) if j >= k else None for j in range(8)]
            pivots = jnp.where(subs == k, row_of[k], pivots)
            inverse = 1.0 / row_of[k]
            whole_row = down(a[p], k)
            for r in range(p, 8):
                m = cols[k][r - p] * inverse
                if r == p:
                    m = jnp.where(subs > k, m, 0.0)
                for j in range(k + 1, 8):
                    cols[j][r - p] = cols[j][r - p] - m * row_of[j]
                a[r] = a[r] - m * whole_row
        done.append(a[p] / jnp.sqrt(pivots))

    both = jnp.concatenate(done, axis=0)
    swapped = pltpu.roll(both, 64, axis=1)
    rows = lax.broadcasted_iota(jnp.int32, (64, 64), 0)
    columns = lax.broadcasted_iota(jnp.int32, (64, 64), 1)
    factor_ref[...] = jnp.where(columns >= rows, both[:, 0:64], 0.0)
    inv = swapped[:, 0:64]
    for j in range(5):
        basis_ref[j] = lax.dot_general(
            inv, adv_ref[j], (((1,), (0,)), ((), ())), precision=HIGHEST, preferred_element_type=F32
        )


def shards(tv, fj, ws, vi, iv, cn, sr, cc):
    nx = lax.axis_size("gx")
    ny = lax.axis_size("gy")
    vmem = pl.BlockSpec(memory_space=pltpu.VMEM)
    block = nx // 4
    team = 2 * block
    per = 32 // team
    hbm = pl.BlockSpec(memory_space=pltpu.HBM)
    adv, gram = pl.pallas_call(
        functools.partial(step_kernel, nx, ny),
        out_shape=(
            jax.ShapeDtypeStruct((5, 64, 128), F32),
            jax.ShapeDtypeStruct((32, 128), F32),
        ),
        in_specs=[hbm] * 7 + [pl.BlockSpec(memory_space=pltpu.SMEM)],
        out_specs=(vmem, vmem),
        scratch_shapes=[
            pltpu.VMEM((5, 64, 128), F32),
            pltpu.SMEM((5, 4, 5), F32),
            pltpu.VMEM((3, 1, 128), F32),
            pltpu.VMEM((4, 128), jnp.int32),
            pltpu.VMEM((4, 16), jnp.int32),
            pltpu.SemaphoreType.DMA((7,)),
            pltpu.VMEM((5, 64, 128), F32),
            pltpu.VMEM((5, 64, 128), F32),
            pltpu.VMEM((8, 128), jnp.int32),
            pltpu.VMEM((64, 128), jnp.int32),
            pltpu.VMEM((4, 64, 128), jnp.int32),
            pltpu.VMEM((4, 5, 5, 8, 128), F32),
            pltpu.VMEM((2, 4, 5, 8, 128), F32),
            pltpu.VMEM((2, 4, 5, 8, 128), F32),
            pltpu.VMEM((team, per, 128), F32),
            pltpu.VMEM((team, per, 128), F32),
            pltpu.VMEM((per, 128), F32),
            pltpu.VMEM((2 * ny, per, 128), F32),
            pltpu.VMEM((per, 128), F32),
            pltpu.VMEM((team, per, 128), F32),
            pltpu.SemaphoreType.REGULAR((4,)),
            pltpu.SemaphoreType.REGULAR((4,)),
            pltpu.SemaphoreType.DMA((4,)),
            pltpu.SemaphoreType.DMA((2, 4)),
            pltpu.SemaphoreType.DMA,
            pltpu.SemaphoreType.DMA,
            pltpu.SemaphoreType.DMA,
            pltpu.SemaphoreType.DMA,
            pltpu.SemaphoreType.DMA,
            pltpu.SemaphoreType.DMA,
        ],
        compiler_params=pltpu.CompilerParams(
            collective_id=0, has_side_effects=True, vmem_limit_bytes=8 << 20
        ),
        name="advance_and_gram",
    )(
        *[
            pltpu.with_memory_space_constraint(v, pltpu.HBM)
            for v in (
                tv,
                fj.transpose(1, 0, 2),
                ws.reshape(1, 128),
                vi.reshape(1, 128),
                iv.reshape(1, 128),
                cn,
                sr,
            )
        ],
        cc,
    )
    return pl.pallas_call(
        factor_kernel,
        out_shape=(
            jax.ShapeDtypeStruct((5, 64, 128), F32),
            jax.ShapeDtypeStruct((64, 64), F32),
        ),
        in_specs=[vmem, vmem],
        out_specs=(vmem, vmem),
        compiler_params=pltpu.CompilerParams(vmem_limit_bytes=8 << 20),
        name="factor_and_apply",
    )(adv, gram)


def solution(mesh):
    cells = P(("gx", "gy"))
    placed = (
        P(None, None, ("gx", "gy")),
        P(),
        cells,
        cells,
        cells,
        P(None, ("gx", "gy")),
        P(None, ("gx", "gy")),
        cells,
    )
    return jax.shard_map(
        shards,
        mesh=mesh,
        in_specs=placed,
        out_specs=(P(None, None, ("gx", "gy")), P()),
        check_vma=False,
    )
```

```python
import functools

import jax
import jax.numpy as jnp
from jax import lax
from jax.experimental import pallas as pl
from jax.experimental.pallas import tpu as pltpu
from jax.sharding import PartitionSpec as P

time_step = 0.4
F32 = jnp.float32
HIGHEST = lax.Precision.HIGHEST
MESH = pl.DeviceIdType.MESH


def pick(x, idx):
    return jnp.take_along_axis(x, idx, axis=1, mode="promise_in_bounds")


def step_kernel(
    nx,
    ny,
    tv_hbm,
    fj_hbm,
    ws_hbm,
    vi_hbm,
    iv_hbm,
    cn_hbm,
    sr_hbm,
    cc_ref,
    adv_ref,
    gram_ref,
    tv_ref,
    fj_ref,
    fac_ref,
    cn_ref,
    sr_ref,
    load_sem,
    w_ref,
    acc_ref,
    pad_ref,
    sidx_ref,
    gidx_ref,
    coef_ref,
    send_ref,
    recv_ref,
    rows_ref,
    part_ref,
    mine_ref,
    line_ref,
    done_ref,
    whole_ref,
    met_x,
    met_y,
    halo_send_sem,
    halo_recv_sem,
    scat_send_sem,
    scat_recv_sem,
    line_send_sem,
    line_recv_sem,
    gath_send_sem,
    gath_recv_sem,
):
    gx = lax.axis_index("gx")
    gy = lax.axis_index("gy")

    def around_x(o):
        return (lax.rem(gx + o + nx, nx), gy)

    def around_y(o):
        return (gx, lax.rem(gy + o + ny, ny))

    block = nx // 4
    place = lax.rem(gx, block)
    row = gx // block
    pair = row // 2
    odd = lax.rem(row, 2)
    flip = pair + odd - 2 * pair * odd
    member = flip * block + place

    barrier = pltpu.get_barrier_semaphore()
    for there in (around_y(1), around_y(-1), around_x(1), around_x(-1)):
        pl.semaphore_signal(barrier, inc=1, device_id=there, device_id_type=MESH)

    loads = [
        pltpu.make_async_copy(src, dst, load_sem.at[k])
        for k, (src, dst) in enumerate(
            (
                (tv_hbm, tv_ref),
                (fj_hbm, fj_ref),
                (ws_hbm, fac_ref.at[0]),
                (vi_hbm, fac_ref.at[1]),
                (iv_hbm, fac_ref.at[2]),
                (cn_hbm, cn_ref),
                (sr_hbm, sr_ref),
            )
        )
    ]
    for k in (6, 5, 0, 2, 3, 4, 1):
        loads[k].start()

    rows = lax.broadcasted_iota(jnp.int32, (64, 128), 0)
    lanes = lax.broadcasted_iota(jnp.int32, (64, 128), 1)
    lanes8 = lax.broadcasted_iota(jnp.int32, (8, 128), 1)
    group8 = lanes8 >> 4
    turn = ((lanes >> 4) - (rows >> 3)) & 7
    base = (rows >> 3) << 4

    pad_ref[...] = jnp.zeros_like(pad_ref)
    loads[6].wait()
    pad_ref[0:4, 0:16] = sr_ref[...]
    send_tile = pick(pad_ref[...], lanes8 & 15)
    send_idx = jnp.zeros((64, 128), jnp.int32)
    for k in range(4):
        tiled = jnp.broadcast_to(send_tile[k : k + 1, :], (64, 128))
        send_idx = jnp.where((turn >> 1) == k, tiled, send_idx)
    sidx_ref[...] = send_idx
    loads[5].wait()
    for f in range(4):
        conn = jnp.broadcast_to(cn_ref[f : f + 1, :], (64, 128))
        slot = conn - 128
        there = base + (((slot >> 4) ^ 1) << 5) + (slot & 15)
        ours = jnp.logical_and(conn >= 128, conn < 192)
        gidx_ref[f] = jnp.where(ours, there, base + 16) & 127

    for k in (0, 2, 3, 4, 1):
        loads[k].wait()
    a_row = -0.5 * fac_ref[0] * fac_ref[2]
    ratio = jnp.broadcast_to(fac_ref[1] / (-0.5 * fac_ref[0]), (8, 128))
    centre = jnp.broadcast_to(-4.0 * ratio[0:1], (64, 128))
    for f in range(4):
        for i in range(5):
            for j in range(5):
                entry = jnp.full((8, 128), fj_ref[i, f, j], F32)
                coef_ref[f, i, j] = entry + ratio if i == j else entry
    w_ref[...] = tv_ref[...]

    def halo(s, k):
        step = 1 if k % 2 else -1
        there = (gx + step, gy) if k < 2 else (gx, gy + step)
        slot = lax.rem(s, 2)
        return pltpu.make_async_remote_copy(
            src_ref=send_ref.at[slot, k],
            dst_ref=recv_ref.at[slot, k],
            send_sem=halo_send_sem.at[k],
            recv_sem=halo_recv_sem.at[slot, k],
            device_id=there,
            device_id_type=MESH,
        )

    sends_to = [gx > 0, gx < nx - 1, gy > 0, gy < ny - 1]
    comes_in = [gx < nx - 1, gx > 0, gy < ny - 1, gy > 0]

    def by_stage(s, values):
        out = values[3]
        for k in (2, 1, 0):
            out = jnp.where(s == k, values[k], out)
        return out

    def stage(s, carry):
        scale = by_stage(s, [F32(time_step / 4), F32(time_step / 3), F32(time_step / 2), F32(time_step)])
        a_fac = jnp.broadcast_to(a_row * scale, (64, 128))
        x = [[None] * 8 for _ in range(5)]
        for g in range(8):
            idx = sidx_ref[8 * g : 8 * g + 8]
            for j in range(5):
                x[j][g] = pick(w_ref[j, 8 * g : 8 * g + 8], idx)
        for j in range(5):
            for k in range(4):
                out = x[j][0]
                for g in range(1, 8):
                    out = jnp.where(group8 == (g + 2 * k) % 8, x[j][g], out)
                send_ref[lax.rem(s, 2), k, j] = out

        @pl.when(s == 0)
        def _():
            pl.semaphore_wait(barrier, 4)

        for k in range(4):

            @pl.when(sends_to[k])
            def _(k=k):
                halo(s, k).start()

        @pl.when(s > 0)
        def _():
            pl.semaphore_wait(met_x.at[s - 1], 2)
            pl.semaphore_wait(met_y.at[s - 1], 2)

        far_x = by_stage(s, [d % nx for d in (1, 2, 4, block)])
        far_y = by_stage(s, [d % ny for d in (1, 2, 4, 8)])
        for o in (far_x, nx - far_x):
            pl.semaphore_signal(met_x.at[s], inc=1, device_id=around_x(o), device_id_type=MESH)
        for o in (far_y, ny - far_y):
            pl.semaphore_signal(met_y.at[s], inc=1, device_id=around_y(o), device_id_type=MESH)

        adv = [None] * 5
        for f in range(4):
            conn = jnp.broadcast_to(cn_ref[f : f + 1, :], (64, 128))
            own = conn < 128
            idx = conn & 127
            for j in range(5):
                n = jnp.where(own, pick(w_ref[j], idx), 0.0)
                for i in range(5):
                    t = jnp.concatenate([coef_ref[f, i, j]] * 8, axis=0) * n
                    adv[i] = t if adv[i] is None else adv[i] + t
        for i in range(5):
            acc_ref[i] = tv_ref[i] + a_fac * (adv[i] + centre * w_ref[i])

        for k in range(4):

            @pl.when(sends_to[k])
            def _(k=k):
                halo(s, k).wait_send()

        for k in range(4):

            @pl.when(comes_in[k])
            def _(k=k):
                halo(s, k).wait_recv()

        for h in range(64 // 8):
            at = pl.ds(8 * h, 8)
            wheel = turn[8 * h : 8 * h + 8]
            ghosts = []
            for j in range(5):
                ghost = jnp.zeros((8, 128), F32)
                for k in range(4):
                    block_of = jnp.concatenate([recv_ref[lax.rem(s, 2), k, j]] * (8 // 8), axis=0)
                    ghost = jnp.where(wheel == 2 * k, block_of, ghost)
                ghosts.append(ghost)
            adv = [None] * 5
            for f in range(4):
                idx = gidx_ref[f, at]
                for j in range(5):
                    n = pick(ghosts[j], idx)
                    for i in range(5):
                        t = jnp.concatenate([coef_ref[f, i, j]] * (8 // 8), axis=0) * n
                        adv[i] = t if adv[i] is None else adv[i] + t
            for i in range(5):
                w_ref[i, at] = acc_ref[i, at] + a_fac[0:8] * adv[i]
        return carry

    lax.fori_loop(0, 4, stage, 0)

    live = lanes < cc_ref[0]
    adv = [jnp.where(live, w_ref[j], 0.0) for j in range(5)]
    for j in range(5):
        adv_ref[j] = adv[j]
    flat = jnp.concatenate(adv, axis=1)
    gram = lax.dot_general(flat, flat, (((1,), (1,)), ((), ())), precision=HIGHEST, preferred_element_type=F32)
    packed = jnp.concatenate([gram[0:32], gram[32:64]], axis=1)
    team = 2 * block
    per = 32 // team
    for r in range(team):
        rows_ref[r] = packed[per * r : per * r + per]
    pl.semaphore_wait(met_x.at[3], 2)
    pl.semaphore_wait(met_y.at[3], 2)

    hops = lambda d, n: min(d, n - d)

    def mate(other, dx, dc):
        core = lax.rem(lax.rem(place, 2) + dc, 2)
        col = lax.rem(place // 2 + dx, block // 2)
        at = col * 2 + core
        to_row = row + 1 - 2 * odd if other else row
        to_flip = 1 - flip if other else flip
        return to_flip * block + at, (to_row * block + at, gy)

    mates = [
        (other, dx, dc) for other in range(2) for dx in range(block // 2) for dc in range(2) if (other, dx, dc) != (0, 0, 0)
    ]
    mates.sort(key=lambda d: -d[0] - hops(d[1], block // 2))

    for d in mates:
        to, there = mate(*d)
        pltpu.make_async_remote_copy(
            src_ref=rows_ref.at[to],
            dst_ref=part_ref.at[member],
            send_sem=scat_send_sem,
            recv_sem=scat_recv_sem,
            device_id=there,
            device_id_type=MESH,
        ).start()
    part_ref[member] = rows_ref[member]
    sized = part_ref.at[pl.ds(1, team - 1)]
    pltpu.make_async_copy(sized, sized, scat_recv_sem).wait()

    def tree(parts):
        while len(parts) > 1:
            parts = [parts[k] + parts[k + 1] if k + 1 < len(parts) else parts[k] for k in range(0, len(parts), 2)]
        return parts[0]

    total = tree([part_ref[r] for r in range(team)])
    mine_ref[...] = total

    here = pair * ny + gy
    others = [(dy, dz) for dy in range(2) for dz in range(ny) if (dy, dz) != (0, 0)]
    others.sort(key=lambda d: -d[0] - hops(d[1], ny))
    for dy, dz in others:
        to_row = 3 - row if dy else row
        pltpu.make_async_remote_copy(
            src_ref=mine_ref,
            dst_ref=line_ref.at[here],
            send_sem=line_send_sem,
            recv_sem=line_recv_sem,
            device_id=(to_row * block + place, lax.rem(gy + dz, ny)),
            device_id_type=MESH,
        ).start()
    line_ref[here] = total
    sized_line = line_ref.at[pl.ds(1, 2 * ny - 1)]
    pltpu.make_async_copy(sized_line, sized_line, line_recv_sem).wait()
    total = tree([line_ref[z] for z in range(2 * ny)])
    total = total / F32(5 * 128 * nx * ny)
    done_ref[...] = total

    for d in mates:
        to, there = mate(*d)
        pltpu.make_async_remote_copy(
            src_ref=done_ref,
            dst_ref=whole_ref.at[member],
            send_sem=gath_send_sem,
            recv_sem=gath_recv_sem,
            device_id=there,
            device_id_type=MESH,
        ).start()
    whole_ref[member] = total
    sized_whole = whole_ref.at[pl.ds(1, team - 1)]
    pltpu.make_async_copy(sized_whole, sized_whole, gath_recv_sem).wait()
    for r in range(team):
        gram_ref[per * r : per * r + per, :] = whole_ref[r]

    pltpu.make_async_copy(sized, sized, scat_send_sem).wait()
    pltpu.make_async_copy(sized_line, sized_line, line_send_sem).wait()
    pltpu.make_async_copy(sized_whole, sized_whole, gath_send_sem).wait()


def factor_kernel(adv_ref, gram_ref, basis_ref, factor_ref):
    lanes = lax.broadcasted_iota(jnp.int32, (8, 128), 1)
    subs = lax.broadcasted_iota(jnp.int32, (8, 128), 0)
    left = lanes < 64
    a = []
    for p in range(8):
        g = gram_ref[8 * (p % 4) : 8 * (p % 4) + 8, :]
        if p >= 4:
            g = pltpu.roll(g, 64, axis=1)
        unit = jnp.where(lanes - 64 == subs + 8 * p, 1.0, 0.0).astype(F32)
        a.append(jnp.where(left, g, unit))

    def across(x, c):
        return jnp.broadcast_to(x[:, c : c + 1], (8, 128))

    def down(x, r):
        return jnp.broadcast_to(x[r : r + 1, :], (8, 128))

    done = []
    for p in range(8):
        cols = [[across(a[r], 8 * p + j) for r in range(p, 8)] for j in range(8)]
        pivots = jnp.ones((8, 128), F32)
        for k in range(8):
            row_of = [down(cols[j][0], k) if j >= k else None for j in range(8)]
            pivots = jnp.where(subs == k, row_of[k], pivots)
            inverse = 1.0 / row_of[k]
            whole_row = down(a[p], k)
            for r in range(p, 8):
                m = cols[k][r - p] * inverse
                if r == p:
                    m = jnp.where(subs > k, m, 0.0)
                for j in range(k + 1, 8):
                    cols[j][r - p] = cols[j][r - p] - m * row_of[j]
                a[r] = a[r] - m * whole_row
        done.append(a[p] / jnp.sqrt(pivots))

    both = jnp.concatenate(done, axis=0)
    swapped = pltpu.roll(both, 64, axis=1)
    rows = lax.broadcasted_iota(jnp.int32, (64, 64), 0)
    columns = lax.broadcasted_iota(jnp.int32, (64, 64), 1)
    factor_ref[...] = jnp.where(columns >= rows, both[:, 0:64], 0.0)
    inv = swapped[:, 0:64]
    for j in range(5):
        basis_ref[j] = lax.dot_general(
            inv, adv_ref[j], (((1,), (0,)), ((), ())), precision=HIGHEST, preferred_element_type=F32
        )


def shards(tv, fj, ws, vi, iv, cn, sr, cc):
    nx = lax.axis_size("gx")
    ny = lax.axis_size("gy")
    vmem = pl.BlockSpec(memory_space=pltpu.VMEM)
    block = nx // 4
    team = 2 * block
    per = 32 // team
    hbm = pl.BlockSpec(memory_space=pltpu.HBM)
    adv, gram = pl.pallas_call(
        functools.partial(step_kernel, nx, ny),
        out_shape=(
            jax.ShapeDtypeStruct((5, 64, 128), F32),
            jax.ShapeDtypeStruct((32, 128), F32),
        ),
        in_specs=[hbm] * 7 + [pl.BlockSpec(memory_space=pltpu.SMEM)],
        out_specs=(vmem, vmem),
        scratch_shapes=[
            pltpu.VMEM((5, 64, 128), F32),
            pltpu.SMEM((5, 4, 5), F32),
            pltpu.VMEM((3, 1, 128), F32),
            pltpu.VMEM((4, 128), jnp.int32),
            pltpu.VMEM((4, 16), jnp.int32),
            pltpu.SemaphoreType.DMA((7,)),
            pltpu.VMEM((5, 64, 128), F32),
            pltpu.VMEM((5, 64, 128), F32),
            pltpu.VMEM((8, 128), jnp.int32),
            pltpu.VMEM((64, 128), jnp.int32),
            pltpu.VMEM((4, 64, 128), jnp.int32),
            pltpu.VMEM((4, 5, 5, 8, 128), F32),
            pltpu.VMEM((2, 4, 5, 8, 128), F32),
            pltpu.VMEM((2, 4, 5, 8, 128), F32),
            pltpu.VMEM((team, per, 128), F32),
            pltpu.VMEM((team, per, 128), F32),
            pltpu.VMEM((per, 128), F32),
            pltpu.VMEM((2 * ny, per, 128), F32),
            pltpu.VMEM((per, 128), F32),
            pltpu.VMEM((team, per, 128), F32),
            pltpu.SemaphoreType.REGULAR((4,)),
            pltpu.SemaphoreType.REGULAR((4,)),
            pltpu.SemaphoreType.DMA((4,)),
            pltpu.SemaphoreType.DMA((2, 4)),
            pltpu.SemaphoreType.DMA,
            pltpu.SemaphoreType.DMA,
            pltpu.SemaphoreType.DMA,
            pltpu.SemaphoreType.DMA,
            pltpu.SemaphoreType.DMA,
            pltpu.SemaphoreType.DMA,
        ],
        compiler_params=pltpu.CompilerParams(
            collective_id=0, has_side_effects=True, vmem_limit_bytes=8 << 20
        ),
        name="advance_and_gram",
    )(
        *[
            pltpu.with_memory_space_constraint(v, pltpu.HBM)
            for v in (
                tv,
                fj.transpose(1, 0, 2),
                ws.reshape(1, 128),
                vi.reshape(1, 128),
                iv.reshape(1, 128),
                cn,
                sr,
            )
        ],
        cc,
    )
    return pl.pallas_call(
        factor_kernel,
        out_shape=(
            jax.ShapeDtypeStruct((5, 64, 128), F32),
            jax.ShapeDtypeStruct((64, 64), F32),
        ),
        in_specs=[vmem, vmem],
        out_specs=(vmem, vmem),
        compiler_params=pltpu.CompilerParams(vmem_limit_bytes=8 << 20),
        name="factor_and_apply",
    )(adv, gram)


def solution(mesh):
    cells = P(("gx", "gy"))
    placed = (
        P(None, None, ("gx", "gy")),
        P(),
        cells,
        cells,
        cells,
        P(None, ("gx", "gy")),
        P(None, ("gx", "gy")),
        cells,
    )
    return jax.shard_map(
        shards,
        mesh=mesh,
        in_specs=placed,
        out_specs=(P(None, None, ("gx", "gy")), P()),
        check_vma=False,
    )
```

```python
import functools

import jax
import jax.numpy as jnp
from jax import lax
from jax.experimental import pallas as pl
from jax.experimental.pallas import tpu as pltpu
from jax.sharding import PartitionSpec as P

time_step = 0.4
F32 = jnp.float32
HIGHEST = lax.Precision.HIGHEST
MESH = pl.DeviceIdType.MESH


def pick(x, idx):
    return jnp.take_along_axis(x, idx, axis=1, mode="promise_in_bounds")


def step_kernel(
    nx,
    ny,
    tv_hbm,
    fj_hbm,
    ws_hbm,
    vi_hbm,
    iv_hbm,
    cn_hbm,
    sr_hbm,
    cc_ref,
    adv_ref,
    gram_ref,
    tv_ref,
    fj_ref,
    fac_ref,
    cn_ref,
    sr_ref,
    load_sem,
    w_ref,
    acc_ref,
    pad_ref,
    sidx_ref,
    gidx_ref,
    coef_ref,
    send_ref,
    recv_ref,
    rows_ref,
    part_ref,
    mine_ref,
    line_ref,
    done_ref,
    whole_ref,
    met_x,
    met_y,
    halo_send_sem,
    halo_recv_sem,
    scat_send_sem,
    scat_recv_sem,
    line_send_sem,
    line_recv_sem,
    gath_send_sem,
    gath_recv_sem,
):
    gx = lax.axis_index("gx")
    gy = lax.axis_index("gy")

    def around_x(o):
        return (lax.rem(gx + o + nx, nx), gy)

    def around_y(o):
        return (gx, lax.rem(gy + o + ny, ny))

    block = nx // 4
    place = lax.rem(gx, block)
    row = gx // block
    pair = row // 2
    odd = lax.rem(row, 2)
    flip = pair + odd - 2 * pair * odd
    member = flip * block + place

    barrier = pltpu.get_barrier_semaphore()
    for there in (around_y(1), around_y(-1), around_x(1), around_x(-1)):
        pl.semaphore_signal(barrier, inc=1, device_id=there, device_id_type=MESH)

    loads = [
        pltpu.make_async_copy(src, dst, load_sem.at[(0, 1, 2, 2, 2, 3, 4)[k]])
        for k, (src, dst) in enumerate(
            (
                (tv_hbm, tv_ref),
                (fj_hbm, fj_ref),
                (ws_hbm, fac_ref.at[0]),
                (vi_hbm, fac_ref.at[1]),
                (iv_hbm, fac_ref.at[2]),
                (cn_hbm, cn_ref),
                (sr_hbm, sr_ref),
            )
        )
    ]
    for k in (6, 5, 0, 2, 3, 4, 1):
        loads[k].start()

    rows = lax.broadcasted_iota(jnp.int32, (64, 128), 0)
    lanes = lax.broadcasted_iota(jnp.int32, (64, 128), 1)
    lanes8 = lax.broadcasted_iota(jnp.int32, (8, 128), 1)
    group8 = lanes8 >> 4
    turn = ((lanes >> 4) - (rows >> 3)) & 7
    base = (rows >> 3) << 4

    pad_ref[...] = jnp.zeros_like(pad_ref)
    loads[6].wait()
    pad_ref[0:4, 0:16] = sr_ref[...]
    send_tile = pick(pad_ref[...], lanes8 & 15)
    send_idx = jnp.zeros((64, 128), jnp.int32)
    for k in range(4):
        tiled = jnp.broadcast_to(send_tile[k : k + 1, :], (64, 128))
        send_idx = jnp.where((turn >> 1) == k, tiled, send_idx)
    sidx_ref[...] = send_idx
    loads[5].wait()
    for f in range(4):
        conn = jnp.broadcast_to(cn_ref[f : f + 1, :], (64, 128))
        slot = conn - 128
        there = base + (((slot >> 4) ^ 1) << 5) + (slot & 15)
        ours = jnp.logical_and(conn >= 128, conn < 192)
        gidx_ref[f] = jnp.where(ours, there, base + 16) & 127

    loads[0].wait()
    loads[1].wait()
    pltpu.make_async_copy(fac_ref, fac_ref, load_sem.at[2]).wait()
    a_row = -0.5 * fac_ref[0] * fac_ref[2]
    ratio = jnp.broadcast_to(fac_ref[1] / (-0.5 * fac_ref[0]), (8, 128))
    centre = jnp.broadcast_to(-4.0 * ratio[0:1], (64, 128))
    for f in range(4):
        for i in range(5):
            for j in range(5):
                entry = jnp.full((8, 128), fj_ref[i, f, j], F32)
                coef_ref[f, i, j] = entry + ratio if i == j else entry
    w_ref[...] = tv_ref[...]

    def halo(s, k):
        step = 1 if k % 2 else -1
        there = (gx + step, gy) if k < 2 else (gx, gy + step)
        slot = lax.rem(s, 2)
        return pltpu.make_async_remote_copy(
            src_ref=send_ref.at[slot, k],
            dst_ref=recv_ref.at[slot, k],
            send_sem=halo_send_sem.at[k],
            recv_sem=halo_recv_sem.at[slot, k],
            device_id=there,
            device_id_type=MESH,
        )

    sends_to = [gx > 0, gx < nx - 1, gy > 0, gy < ny - 1]
    comes_in = [gx < nx - 1, gx > 0, gy < ny - 1, gy > 0]

    def by_stage(s, values):
        out = values[3]
        for k in (2, 1, 0):
            out = jnp.where(s == k, values[k], out)
        return out

    def stage(s, carry):
        scale = by_stage(s, [F32(time_step / 4), F32(time_step / 3), F32(time_step / 2), F32(time_step)])
        a_fac = jnp.broadcast_to(a_row * scale, (64, 128))
        x = [[None] * 8 for _ in range(5)]
        for g in range(8):
            idx = sidx_ref[8 * g : 8 * g + 8]
            for j in range(5):
                x[j][g] = pick(w_ref[j, 8 * g : 8 * g + 8], idx)
        for j in range(5):
            for k in range(4):
                out = x[j][0]
                for g in range(1, 8):
                    out = jnp.where(group8 == (g + 2 * k) % 8, x[j][g], out)
                send_ref[lax.rem(s, 2), k, j] = out

        @pl.when(s == 0)
        def _():
            pl.semaphore_wait(barrier, 4)

        for k in range(4):

            @pl.when(sends_to[k])
            def _(k=k):
                halo(s, k).start()

        @pl.when(s > 0)
        def _():
            pl.semaphore_wait(met_x.at[jnp.maximum(s - 1, 0)], 2)
            pl.semaphore_wait(met_y.at[jnp.maximum(s - 1, 0)], 2)

        far_x = by_stage(s, [d % nx for d in (1, 2, 4, block)])
        far_y = by_stage(s, [d % ny for d in (1, 2, 4, 8)])
        for o in (far_x, nx - far_x):
            pl.semaphore_signal(met_x.at[s], inc=1, device_id=around_x(o), device_id_type=MESH)
        for o in (far_y, ny - far_y):
            pl.semaphore_signal(met_y.at[s], inc=1, device_id=around_y(o), device_id_type=MESH)

        adv = [None] * 5
        for f in range(4):
            conn = jnp.broadcast_to(cn_ref[f : f + 1, :], (64, 128))
            own = conn < 128
            idx = conn & 127
            for j in range(5):
                n = jnp.where(own, pick(w_ref[j], idx), 0.0)
                for i in range(5):
                    t = jnp.concatenate([coef_ref[f, i, j]] * 8, axis=0) * n
                    adv[i] = t if adv[i] is None else adv[i] + t
        for i in range(5):
            acc_ref[i] = tv_ref[i] + a_fac * (adv[i] + centre * w_ref[i])

        for k in range(4):

            @pl.when(sends_to[k])
            def _(k=k):
                halo(s, k).wait_send()

        for k in range(4):

            @pl.when(comes_in[k])
            def _(k=k):
                halo(s, k).wait_recv()

        for h in range(64 // 8):
            at = pl.ds(8 * h, 8)
            wheel = turn[8 * h : 8 * h + 8]
            ghosts = []
            for j in range(5):
                ghost = jnp.zeros((8, 128), F32)
                for k in range(4):
                    block_of = jnp.concatenate([recv_ref[lax.rem(s, 2), k, j]] * (8 // 8), axis=0)
                    ghost = jnp.where(wheel == 2 * k, block_of, ghost)
                ghosts.append(ghost)
            adv = [None] * 5
            for f in range(4):
                idx = gidx_ref[f, at]
                for j in range(5):
                    n = pick(ghosts[j], idx)
                    for i in range(5):
                        t = jnp.concatenate([coef_ref[f, i, j]] * (8 // 8), axis=0) * n
                        adv[i] = t if adv[i] is None else adv[i] + t
            for i in range(5):
                w_ref[i, at] = acc_ref[i, at] + a_fac[0:8] * adv[i]
        return carry

    lax.fori_loop(0, 4, stage, 0)

    live = lanes < cc_ref[0]
    adv = [jnp.where(live, w_ref[j], 0.0) for j in range(5)]
    for j in range(5):
        adv_ref[j] = adv[j]
    flat = jnp.concatenate(adv, axis=1)
    gram = lax.dot_general(flat, flat, (((1,), (1,)), ((), ())), precision=HIGHEST, preferred_element_type=F32)
    packed = jnp.concatenate([gram[0:32], gram[32:64]], axis=1)
    team = 2 * block
    per = 32 // team
    for r in range(team):
        rows_ref[r] = packed[per * r : per * r + per]
    pl.semaphore_wait(met_x.at[3], 2)
    pl.semaphore_wait(met_y.at[3], 2)

    hops = lambda d, n: min(d, n - d)

    def mate(other, dx, dc):
        core = lax.rem(lax.rem(place, 2) + dc, 2)
        col = lax.rem(place // 2 + dx, block // 2)
        at = col * 2 + core
        to_row = row + 1 - 2 * odd if other else row
        to_flip = 1 - flip if other else flip
        return to_flip * block + at, (to_row * block + at, gy)

    mates = [
        (other, dx, dc) for other in range(2) for dx in range(block // 2) for dc in range(2) if (other, dx, dc) != (0, 0, 0)
    ]
    mates.sort(key=lambda d: -d[0] - hops(d[1], block // 2))

    for d in mates:
        to, there = mate(*d)
        pltpu.make_async_remote_copy(
            src_ref=rows_ref.at[to],
            dst_ref=part_ref.at[member],
            send_sem=scat_send_sem,
            recv_sem=scat_recv_sem,
            device_id=there,
            device_id_type=MESH,
        ).start()
    part_ref[member] = rows_ref[member]
    sized = part_ref.at[pl.ds(1, team - 1)]
    pltpu.make_async_copy(sized, sized, scat_recv_sem).wait()

    def tree(parts):
        while len(parts) > 1:
            parts = [parts[k] + parts[k + 1] if k + 1 < len(parts) else parts[k] for k in range(0, len(parts), 2)]
        return parts[0]

    total = tree([part_ref[r] for r in range(team)])
    mine_ref[...] = total

    here = pair * ny + gy
    others = [(dy, dz) for dy in range(2) for dz in range(ny) if (dy, dz) != (0, 0)]
    others.sort(key=lambda d: -d[0] - hops(d[1], ny))
    for dy, dz in others:
        to_row = 3 - row if dy else row
        pltpu.make_async_remote_copy(
            src_ref=mine_ref,
            dst_ref=line_ref.at[here],
            send_sem=line_send_sem,
            recv_sem=line_recv_sem,
            device_id=(to_row * block + place, lax.rem(gy + dz, ny)),
            device_id_type=MESH,
        ).start()
    line_ref[here] = total
    sized_line = line_ref.at[pl.ds(1, 2 * ny - 1)]
    pltpu.make_async_copy(sized_line, sized_line, line_recv_sem).wait()
    total = tree([line_ref[z] for z in range(2 * ny)])
    total = total / F32(5 * 128 * nx * ny)
    done_ref[...] = total

    for d in mates:
        to, there = mate(*d)
        pltpu.make_async_remote_copy(
            src_ref=done_ref,
            dst_ref=whole_ref.at[member],
            send_sem=gath_send_sem,
            recv_sem=gath_recv_sem,
            device_id=there,
            device_id_type=MESH,
        ).start()
    whole_ref[member] = total
    sized_whole = whole_ref.at[pl.ds(1, team - 1)]
    pltpu.make_async_copy(sized_whole, sized_whole, gath_recv_sem).wait()
    for r in range(team):
        gram_ref[per * r : per * r + per, :] = whole_ref[r]

    pltpu.make_async_copy(sized, sized, scat_send_sem).wait()
    pltpu.make_async_copy(sized_line, sized_line, line_send_sem).wait()
    pltpu.make_async_copy(sized_whole, sized_whole, gath_send_sem).wait()


def factor_kernel(adv_ref, gram_ref, basis_ref, factor_ref):
    lanes = lax.broadcasted_iota(jnp.int32, (8, 128), 1)
    subs = lax.broadcasted_iota(jnp.int32, (8, 128), 0)
    left = lanes < 64
    a = []
    for p in range(8):
        g = gram_ref[8 * (p % 4) : 8 * (p % 4) + 8, :]
        if p >= 4:
            g = pltpu.roll(g, 64, axis=1)
        unit = jnp.where(lanes - 64 == subs + 8 * p, 1.0, 0.0).astype(F32)
        a.append(jnp.where(left, g, unit))

    def across(x, c):
        return jnp.broadcast_to(x[:, c : c + 1], (8, 128))

    def down(x, r):
        return jnp.broadcast_to(x[r : r + 1, :], (8, 128))

    done = []
    for p in range(8):
        cols = [[across(a[r], 8 * p + j) for r in range(p, 8)] for j in range(8)]
        pivots = jnp.ones((8, 128), F32)
        for k in range(8):
            row_of = [down(cols[j][0], k) if j >= k else None for j in range(8)]
            pivots = jnp.where(subs == k, row_of[k], pivots)
            inverse = 1.0 / row_of[k]
            whole_row = down(a[p], k)
            for r in range(p, 8):
                m = cols[k][r - p] * inverse
                if r == p:
                    m = jnp.where(subs > k, m, 0.0)
                for j in range(k + 1, 8):
                    cols[j][r - p] = cols[j][r - p] - m * row_of[j]
                a[r] = a[r] - m * whole_row
        done.append(a[p] / jnp.sqrt(pivots))

    both = jnp.concatenate(done, axis=0)
    swapped = pltpu.roll(both, 64, axis=1)
    rows = lax.broadcasted_iota(jnp.int32, (64, 64), 0)
    columns = lax.broadcasted_iota(jnp.int32, (64, 64), 1)
    factor_ref[...] = jnp.where(columns >= rows, both[:, 0:64], 0.0)
    inv = swapped[:, 0:64]
    for j in range(5):
        basis_ref[j] = lax.dot_general(
            inv, adv_ref[j], (((1,), (0,)), ((), ())), precision=HIGHEST, preferred_element_type=F32
        )


def shards(tv, fj, ws, vi, iv, cn, sr, cc):
    nx = lax.axis_size("gx")
    ny = lax.axis_size("gy")
    vmem = pl.BlockSpec(memory_space=pltpu.VMEM)
    block = nx // 4
    team = 2 * block
    per = 32 // team
    hbm = pl.BlockSpec(memory_space=pltpu.HBM)
    adv, gram = pl.pallas_call(
        functools.partial(step_kernel, nx, ny),
        out_shape=(
            jax.ShapeDtypeStruct((5, 64, 128), F32),
            jax.ShapeDtypeStruct((32, 128), F32),
        ),
        in_specs=[hbm] * 7 + [pl.BlockSpec(memory_space=pltpu.SMEM)],
        out_specs=(vmem, vmem),
        scratch_shapes=[
            pltpu.VMEM((5, 64, 128), F32),
            pltpu.SMEM((5, 4, 5), F32),
            pltpu.VMEM((3, 1, 128), F32),
            pltpu.VMEM((4, 128), jnp.int32),
            pltpu.VMEM((4, 16), jnp.int32),
            pltpu.SemaphoreType.DMA((5,)),
            pltpu.VMEM((5, 64, 128), F32),
            pltpu.VMEM((5, 64, 128), F32),
            pltpu.VMEM((8, 128), jnp.int32),
            pltpu.VMEM((64, 128), jnp.int32),
            pltpu.VMEM((4, 64, 128), jnp.int32),
            pltpu.VMEM((4, 5, 5, 8, 128), F32),
            pltpu.VMEM((2, 4, 5, 8, 128), F32),
            pltpu.VMEM((2, 4, 5, 8, 128), F32),
            pltpu.VMEM((team, per, 128), F32),
            pltpu.VMEM((team, per, 128), F32),
            pltpu.VMEM((per, 128), F32),
            pltpu.VMEM((2 * ny, per, 128), F32),
            pltpu.VMEM((per, 128), F32),
            pltpu.VMEM((team, per, 128), F32),
            pltpu.SemaphoreType.REGULAR((4,)),
            pltpu.SemaphoreType.REGULAR((4,)),
            pltpu.SemaphoreType.DMA((4,)),
            pltpu.SemaphoreType.DMA((2, 4)),
            pltpu.SemaphoreType.DMA,
            pltpu.SemaphoreType.DMA,
            pltpu.SemaphoreType.DMA,
            pltpu.SemaphoreType.DMA,
            pltpu.SemaphoreType.DMA,
            pltpu.SemaphoreType.DMA,
        ],
        compiler_params=pltpu.CompilerParams(
            collective_id=0, has_side_effects=True, vmem_limit_bytes=8 << 20
        ),
        name="advance_and_gram",
    )(
        *[
            pltpu.with_memory_space_constraint(v, pltpu.HBM)
            for v in (
                tv,
                fj.transpose(1, 0, 2),
                ws.reshape(1, 128),
                vi.reshape(1, 128),
                iv.reshape(1, 128),
                cn,
                sr,
            )
        ],
        cc,
    )
    return pl.pallas_call(
        factor_kernel,
        out_shape=(
            jax.ShapeDtypeStruct((5, 64, 128), F32),
            jax.ShapeDtypeStruct((64, 64), F32),
        ),
        in_specs=[vmem, vmem],
        out_specs=(vmem, vmem),
        compiler_params=pltpu.CompilerParams(vmem_limit_bytes=8 << 20),
        name="factor_and_apply",
    )(adv, gram)


def solution(mesh):
    cells = P(("gx", "gy"))
    placed = (
        P(None, None, ("gx", "gy")),
        P(),
        cells,
        cells,
        cells,
        P(None, ("gx", "gy")),
        P(None, ("gx", "gy")),
        cells,
    )
    return jax.shard_map(
        shards,
        mesh=mesh,
        in_specs=placed,
        out_specs=(P(None, None, ("gx", "gy")), P()),
        check_vma=False,
    )
```
